256 devices in a mesh: grp: 4 (over x), dev: 64 (over y, z, core).
Axes of the slice: x: 4, y: 4, z: 8, core: 2. Of those that a mesh axis runs over, the one named last changes fastest.
Arguments:
- points: bfloat16 [524288, 256], P(('grp', 'dev')), may hold values from -6 to 6
- ridge: float32 [1024], replicated, may hold values from 0.25 to 2
- landmark_ids: int32 [1024], replicated, may hold values from 0 to 524287, as said below
Outputs:
- features: bfloat16 [524288, 1024], P(('grp', 'dev'))
The draws below stay inside these ranges and needn't reach their ends.
Inputs may be any that keep to these rules, and one draw needn't show every extreme that they name: `landmark_ids`: sorted ascending, all distinct.
All inputs are finite; a program needn't handle non-finite values.
Results may differ from the reference program's by a relative error of at most 0.0015.
Values may be sent and summed in bfloat16 or wider, within the bound.
A program may use at most 128 MiB of HBM per device.

```python
import math
import jax
import jax.numpy as jnp
from jax import lax

D = 256
M = 1024
ROWS = 2048
NPTS = 524288


def draw_landmark_ids(key, part):
    order = jax.random.permutation(jax.random.fold_in(key, 11), NPTS)
    return jnp.sort(order[:M]).astype(jnp.int32)


def block_levels(rng, dims, split, low, largest):
    level = 1.0
    for dim, parts in split:
        steps = jax.random.uniform(jax.random.fold_in(jax.random.fold_in(rng, 6), dim), (parts,), jnp.float32, low / len(split), largest / len(split))
        level = level * jnp.repeat(jnp.exp(steps), dims[dim] // parts).reshape((-1,) + (1,) * (len(dims) - 1 - dim))
    return level


def gaussian(rng, shape, deviation, limit, shards=(), dtype=jnp.bfloat16):
    values = deviation * jax.random.normal(rng, shape, jnp.float32)
    if shards:
        values = values * block_levels(rng, shape, shards, -0.22, 0.18)
    return jnp.clip(values, -limit, limit).astype(dtype)


def setup_inputs(seed: int = 0) -> dict:
    seeds = jax.random.split(jax.random.key(seed), 4)
    return {
        "points": gaussian(seeds[0], (NPTS, D), 1.0, 6.0, ((0, 256),)),
        "ridge": jnp.clip(jnp.exp(jax.random.uniform(seeds[1], (M,), jnp.float32, math.log(0.25), math.log(2.0))), 0.25, 2.0),
        "landmark_ids": draw_landmark_ids(jax.random.fold_in(seeds[3], 71), 0),
    }


def kernel_block(left, right):
    left_sq = lax.optimization_barrier(jnp.sum(jnp.square(left.astype(jnp.float32)), axis=1))
    right_sq = lax.optimization_barrier(jnp.sum(jnp.square(right.astype(jnp.float32)), axis=1))
    inner = jnp.dot(left.astype(jnp.float32), right.T.astype(jnp.float32), preferred_element_type=jnp.float32)
    return jnp.exp(-(left_sq[:, None] + right_sq[None, :] - 2.0 * inner) / (2.0 * D))

def reference(points, ridge, landmark_ids):
    marks = points[landmark_ids.astype(jnp.int32)]
    core = kernel_block(marks, marks) + jnp.diag(ridge)
    lower = jnp.linalg.cholesky(core)

    def one_block(block):
        cross = kernel_block(block, marks)
        return lax.linalg.triangular_solve(lower, cross, left_side=False, lower=True, transpose_a=True)
    blocks = points.reshape(NPTS // ROWS, ROWS, D)
    raw = lax.map(one_block, blocks).reshape(NPTS, M)
    mean = lax.optimization_barrier(jnp.mean(raw, axis=0))
    var = lax.optimization_barrier(jnp.mean(jnp.square(raw - mean[None, :]), axis=0))
    return ((raw - mean[None, :]) / jnp.sqrt(var + 1e-05)[None, :]).astype(jnp.bfloat16)
```

```python
import functools

import jax
import jax.numpy as jnp
from jax import lax
from jax.experimental import pallas as pl
from jax.experimental.pallas import tpu as pltpu
from jax.sharding import Mesh
from jax.sharding import PartitionSpec as P

GRP_DEV = ("grp", "dev_0", "dev_1", "dev_2")
F32 = jnp.float32
BF16 = jnp.bfloat16
HI = lax.Precision.HIGHEST
BLK = 128
ROWS_STEP = 256
VMEM = pl.BlockSpec(memory_space=pltpu.VMEM)


def lane(x, c):
    return jnp.broadcast_to(x[:, c : c + 1], (8, 128))


def sub(x, k):
    return jnp.broadcast_to(x[k : k + 1, :], (8, 128))


def eliminate64(g1, g2, lane0):
    row = lax.broadcasted_iota(jnp.int32, (8, 128), 0)
    for q in range(8):
        b = [[lane(g1[t], lane0 + 8 * q + c) for t in range(q, 8)] for c in range(8)]
        scale = None
        for k in range(8):
            p = sub(b[k][0], k)
            r = 1.0 / p
            rs = lax.rsqrt(p)
            scale = rs if scale is None else jnp.where(row == k, rs, scale)
            m = [x * r for x in b[k]]
            m[0] = jnp.where(row > k, m[0], 0.0)
            for c in range(k + 1, 8):
                a = sub(b[c][0], k)
                b[c] = [x - y * a for x, y in zip(b[c], m)]
            a1 = sub(g1[q], k)
            a2 = sub(g2[q], k)
            for t in range(q, 8):
                g1[t] = g1[t] - m[t - q] * a1
                g2[t] = g2[t] - m[t - q] * a2
        g1[q] = g1[q] * scale
        g2[q] = g2[q] * scale
    return g1, g2


def dot(a, b):
    return jnp.dot(a, b, preferred_element_type=F32, precision=HI)


def inverse_factor(s, eye):
    rows = lambda x: [x[8 * t : 8 * t + 8] for t in range(8)]
    u, v = eliminate64(rows(s[:64]), rows(eye[:64]), 0)
    u = jnp.concatenate(u, 0)
    v = jnp.concatenate(v, 0)
    ut = u.T[64:128]
    _, v2 = eliminate64(rows(s[64:] - dot(ut, u)), rows(eye[64:] - dot(ut, v)), 64)
    return jnp.concatenate([v] + v2, 0)


def split(x):
    high = x.astype(BF16)
    return high, (x - high.astype(F32)).astype(BF16)


def factor_kernel(marks_ref, ridge_ref, hi_ref, lo_ref, norm_ref, m):
    n, d = marks_ref.shape
    nb = n // BLK
    eye = (
        lax.broadcasted_iota(jnp.int32, (BLK, BLK), 0)
        == lax.broadcasted_iota(jnp.int32, (BLK, BLK), 1)
    ).astype(F32)
    sq = jnp.square(marks_ref[...].astype(F32))
    nr = lax.dot_general(
        jnp.ones((8, d), F32), sq, (((1,), (1,)), ((), ())), preferred_element_type=F32, precision=HI
    )
    norm_ref[...] = nr
    for i in range(nb):
        rows = slice(i * BLK, (i + 1) * BLK)
        blk = marks_ref[rows, :]
        nc = jnp.sum(jnp.square(blk.astype(F32)), axis=1, keepdims=True)
        g = lax.dot_general(blk, marks_ref[...], (((1,), (1,)), ((), ())), preferred_element_type=F32)
        m[rows, :] = jnp.exp((2.0 * g - nc - nr[:1]) * (1.0 / (2.0 * d)))
        m[rows, rows] += eye * ridge_ref[:, rows]

    def step(j, carry):
        o = pl.multiple_of(j * BLK, BLK)
        linv = inverse_factor(m[pl.ds(o, BLK), pl.ds(o, BLK)], eye)
        m[pl.ds(o, BLK), pl.ds(o, BLK)] = eye
        m[pl.ds(o, BLK), :] = dot(linv, m[pl.ds(o, BLK), :])

        def update(i, carry):
            p = pl.multiple_of(i * BLK, BLK)
            ut = m[pl.ds(o, BLK), pl.ds(p, BLK)].T
            m[pl.ds(p, BLK), pl.ds(o, BLK)] = jnp.zeros((BLK, BLK), F32)
            m[pl.ds(p, BLK), :] = m[pl.ds(p, BLK), :] - dot(ut, m[pl.ds(o, BLK), :])
            return carry

        return lax.fori_loop(j + 1, nb, update, carry)

    lax.fori_loop(0, nb, step, 0)
    for i in range(nb):
        rows = slice(i * BLK, (i + 1) * BLK)
        x = m[rows, :]
        x = jnp.where(lax.broadcasted_iota(jnp.int32, x.shape, 1) < (i + 1) * BLK, x, 0.0)
        hi_ref[rows, :], lo_ref[rows, :] = split(x)


def factor(marks, ridge):
    n = marks.shape[0]
    return pl.pallas_call(
        factor_kernel,
        out_shape=[
            jax.ShapeDtypeStruct((n, n), BF16),
            jax.ShapeDtypeStruct((n, n), BF16),
            jax.ShapeDtypeStruct((8, n), F32),
        ],
        in_specs=[VMEM, VMEM],
        out_specs=[VMEM, VMEM, VMEM],
        scratch_shapes=[pltpu.VMEM((n, n), F32)],
        name="factor",
        compiler_params=pltpu.CompilerParams(vmem_limit_bytes=40 << 20),
    )(marks, ridge.reshape(1, n))


def raw_kernel(points_ref, marks_ref, norm_ref, hi_ref, lo_ref, raw_ref, stats_ref):
    d = points_ref.shape[1]
    n = marks_ref.shape[0]
    pts = points_ref[...]
    nc = jnp.sum(jnp.square(pts.astype(F32)), axis=1, keepdims=True)
    g = lax.dot_general(pts, marks_ref[...], (((1,), (1,)), ((), ())), preferred_element_type=F32)
    ch, cl = split(jnp.exp((2.0 * g - nc - norm_ref[:1, :]) * (1.0 / (2.0 * d))))

    @pl.when(pl.program_id(0) == 0)
    def _():
        stats_ref[...] = jnp.zeros_like(stats_ref)

    for j in range(n // 256):
        cols = slice(j * 256, (j + 1) * 256)
        k = (j + 1) * 256
        mul = lambda a, b: lax.dot_general(
            a, b, (((1,), (1,)), ((), ())), preferred_element_type=F32
        )
        x = mul(ch[:, :k], hi_ref[cols, :k])
        x += mul(cl[:, :k], hi_ref[cols, :k])
        x += mul(ch[:, :k], lo_ref[cols, :k])
        raw_ref[:, cols] = x
        stats_ref[0:1, cols] += jnp.sum(x, axis=0, keepdims=True)
        stats_ref[1:2, cols] += jnp.sum(jnp.square(x), axis=0, keepdims=True)


def raw_features(points, marks, norms, hi, lo):
    rows, d = points.shape
    n = marks.shape[0]
    whole = lambda shape: pl.BlockSpec(shape, lambda i: (0, 0), pipeline_mode=pl.Buffered(1))
    return pl.pallas_call(
        raw_kernel,
        grid=(rows // ROWS_STEP,),
        out_shape=[jax.ShapeDtypeStruct((rows, n), F32), jax.ShapeDtypeStruct((8, n), F32)],
        in_specs=[
            pl.BlockSpec((ROWS_STEP, d), lambda i: (i, 0)),
            whole((n, d)),
            whole((8, n)),
            whole((n, n)),
            whole((n, n)),
        ],
        out_specs=[
            pl.BlockSpec((ROWS_STEP, n), lambda i: (i, 0)),
            pl.BlockSpec((8, n), lambda i: (0, 0)),
        ],
        name="raw",
        compiler_params=pltpu.CompilerParams(vmem_limit_bytes=40 << 20),
    )(points, marks, norms, hi, lo)


def shards(points, ridge, landmark_ids):
    count = points.shape[0]
    start = lax.axis_index(GRP_DEV) * count
    offset = landmark_ids - start
    inside = (offset >= 0) & (offset < count)
    picked = points[jnp.clip(offset, 0, count - 1)]
    filled = jnp.where(inside[:, None], picked, jnp.zeros((), BF16))
    marks = lax.psum(filled, GRP_DEV)
    hi, lo, norms = factor(marks, ridge)
    raw, stats = raw_features(points, marks, norms, hi, lo)
    total_rows = count * lax.axis_size(GRP_DEV)
    stats = lax.psum(stats[:2], GRP_DEV) / total_rows
    mean, var = stats[0], jnp.maximum(stats[1] - jnp.square(stats[0]), 0.0)
    return ((raw - mean[None, :]) * lax.rsqrt(var + 1e-05)[None, :]).astype(BF16)


def solution(mesh):
    torus = Mesh(
        mesh.devices.reshape(mesh.shape["grp"], 4, 8, 2), ("grp", "dev_0", "dev_1", "dev_2")
    )
    placed = (P(GRP_DEV, None), P(), P())
    return jax.shard_map(
        shards, mesh=torus, in_specs=placed, out_specs=P(GRP_DEV, None), check_vma=False
    )
```

```python
import functools

import jax
import jax.numpy as jnp
from jax import lax
from jax.experimental import pallas as pl
from jax.experimental.pallas import tpu as pltpu
from jax.sharding import Mesh
from jax.sharding import PartitionSpec as P

GRP_DEV = ("grp", "dev_0", "dev_1", "dev_2")
F32 = jnp.float32
BF16 = jnp.bfloat16
HI = lax.Precision.HIGHEST
BLK = 128
ROWS_STEP = 256
VMEM = pl.BlockSpec(memory_space=pltpu.VMEM)


def lane(x, c):
    return jnp.broadcast_to(x[:, c : c + 1], (8, 128))


def sub(x, k):
    return jnp.broadcast_to(x[k : k + 1, :], (8, 128))


def eliminate64(g1, g2, lane0):
    row = lax.broadcasted_iota(jnp.int32, (8, 128), 0)
    for q in range(8):
        b = [[lane(g1[t], lane0 + 8 * q + c) for t in range(q, 8)] for c in range(8)]
        scale = None
        for k in range(8):
            p = sub(b[k][0], k)
            r = 1.0 / p
            rs = lax.rsqrt(p)
            scale = rs if scale is None else jnp.where(row == k, rs, scale)
            m = [x * r for x in b[k]]
            m[0] = jnp.where(row > k, m[0], 0.0)
            for c in range(k + 1, 8):
                a = sub(b[c][0], k)
                b[c] = [x - y * a for x, y in zip(b[c], m)]
            a1 = sub(g1[q], k)
            a2 = sub(g2[q], k)
            for t in range(q, 8):
                g1[t] = g1[t] - m[t - q] * a1
                g2[t] = g2[t] - m[t - q] * a2
        g1[q] = g1[q] * scale
        g2[q] = g2[q] * scale
    return g1, g2


def dot(a, b):
    return jnp.dot(a, b, preferred_element_type=F32, precision=HI)


def inverse_factor(s, eye):
    rows = lambda x: [x[8 * t : 8 * t + 8] for t in range(8)]
    u, v = eliminate64(rows(s[:64]), rows(eye[:64]), 0)
    u = jnp.concatenate(u, 0)
    v = jnp.concatenate(v, 0)
    ut = u.T[64:128]
    _, v2 = eliminate64(rows(s[64:] - dot(ut, u)), rows(eye[64:] - dot(ut, v)), 64)
    return jnp.concatenate([v] + v2, 0)


def split(x):
    high = x.astype(BF16)
    return high, (x - high.astype(F32)).astype(BF16)


def factor_kernel(marks_ref, ridge_ref, hi_ref, lo_ref, norm_ref, m):
    n, d = marks_ref.shape
    nb = n // BLK
    eye = (
        lax.broadcasted_iota(jnp.int32, (BLK, BLK), 0)
        == lax.broadcasted_iota(jnp.int32, (BLK, BLK), 1)
    ).astype(F32)
    sq = jnp.square(marks_ref[...].astype(F32))
    nr = lax.dot_general(
        jnp.ones((8, d), F32), sq, (((1,), (1,)), ((), ())), preferred_element_type=F32, precision=HI
    )
    norm_ref[...] = nr
    for i in range(nb):
        rows = slice(i * BLK, (i + 1) * BLK)
        blk = marks_ref[rows, :]
        nc = jnp.sum(jnp.square(blk.astype(F32)), axis=1, keepdims=True)
        g = lax.dot_general(blk, marks_ref[...], (((1,), (1,)), ((), ())), preferred_element_type=F32)
        m[rows, :] = jnp.exp((2.0 * g - nc - nr[:1]) * (1.0 / (2.0 * d)))
        m[rows, rows] += eye * ridge_ref[:, rows]

    def step(j, carry):
        o = pl.multiple_of(j * BLK, BLK)
        linv = inverse_factor(m[pl.ds(o, BLK), pl.ds(o, BLK)], eye)
        m[pl.ds(o, BLK), pl.ds(o, BLK)] = eye
        m[pl.ds(o, BLK), :] = dot(linv, m[pl.ds(o, BLK), :])

        def update(i, carry):
            p = pl.multiple_of(i * BLK, BLK)
            ut = m[pl.ds(o, BLK), pl.ds(p, BLK)].T
            m[pl.ds(p, BLK), pl.ds(o, BLK)] = jnp.zeros((BLK, BLK), F32)
            m[pl.ds(p, BLK), :] = m[pl.ds(p, BLK), :] - dot(ut, m[pl.ds(o, BLK), :])
            return carry

        return lax.fori_loop(j + 1, nb, update, carry)

    lax.fori_loop(0, nb, step, 0)
    for i in range(nb):
        rows = slice(i * BLK, (i + 1) * BLK)
        x = m[rows, :]
        x = jnp.where(lax.broadcasted_iota(jnp.int32, x.shape, 1) < (i + 1) * BLK, x, 0.0)
        hi_ref[rows, :], lo_ref[rows, :] = split(x)


def factor(marks, ridge):
    n = marks.shape[0]
    return pl.pallas_call(
        factor_kernel,
        out_shape=[
            jax.ShapeDtypeStruct((n, n), BF16),
            jax.ShapeDtypeStruct((n, n), BF16),
            jax.ShapeDtypeStruct((8, n), F32),
        ],
        in_specs=[VMEM, VMEM],
        out_specs=[VMEM, VMEM, VMEM],
        scratch_shapes=[pltpu.VMEM((n, n), F32)],
        name="factor",
        compiler_params=pltpu.CompilerParams(vmem_limit_bytes=40 << 20),
    )(marks, ridge.reshape(1, n))


def raw_kernel(points_ref, marks_ref, norm_ref, hi_ref, lo_ref, raw_ref, stats_ref):
    d = points_ref.shape[1]
    n = marks_ref.shape[0]
    pts = points_ref[...]
    nc = jnp.sum(jnp.square(pts.astype(F32)), axis=1, keepdims=True)
    g = lax.dot_general(pts, marks_ref[...], (((1,), (1,)), ((), ())), preferred_element_type=F32)
    ch, cl = split(jnp.exp((2.0 * g - nc - norm_ref[:1, :]) * (1.0 / (2.0 * d))))

    @pl.when(pl.program_id(0) == 0)
    def _():
        stats_ref[...] = jnp.zeros_like(stats_ref)

    for j in range(n // 256):
        cols = slice(j * 256, (j + 1) * 256)
        k = (j + 1) * 256
        mul = lambda a, b: lax.dot_general(
            a, b, (((1,), (1,)), ((), ())), preferred_element_type=F32
        )
        x = mul(ch[:, :k], hi_ref[cols, :k])
        x += mul(cl[:, :k], hi_ref[cols, :k])
        x += mul(ch[:, :k], lo_ref[cols, :k])
        raw_ref[:, cols] = x
        for i in range(2):
            y = x[:, i * 128 : (i + 1) * 128]
            r = 2 * j + i
            stats_ref[r : r + 1, :] += jnp.sum(y, axis=0, keepdims=True)
            stats_ref[8 + r : 9 + r, :] += jnp.sum(jnp.square(y), axis=0, keepdims=True)


def raw_features(points, marks, norms, hi, lo):
    rows, d = points.shape
    n = marks.shape[0]
    whole = lambda shape: pl.BlockSpec(shape, lambda i: (0, 0), pipeline_mode=pl.Buffered(1))
    return pl.pallas_call(
        raw_kernel,
        grid=(rows // ROWS_STEP,),
        out_shape=[jax.ShapeDtypeStruct((rows, n), F32), jax.ShapeDtypeStruct((16, n // 8), F32)],
        in_specs=[
            pl.BlockSpec((ROWS_STEP, d), lambda i: (i, 0)),
            whole((n, d)),
            whole((8, n)),
            whole((n, n)),
            whole((n, n)),
        ],
        out_specs=[
            pl.BlockSpec((ROWS_STEP, n), lambda i: (i, 0)),
            pl.BlockSpec((16, n // 8), lambda i: (0, 0)),
        ],
        name="raw",
        compiler_params=pltpu.CompilerParams(vmem_limit_bytes=40 << 20),
    )(points, marks, norms, hi, lo)


MESH_IDS = pl.DeviceIdType.MESH
SLOTS = 16
WINDOW = 128
DMA = pltpu.SemaphoreType.DMA


def position():
    inner = lax.axis_index("dev_1") * 2 + lax.axis_index("dev_2")
    outer = lax.axis_index("grp") * 4 + lax.axis_index("dev_0")
    return inner, outer


def inner_peer(i):
    return {"dev_1": lax.div(i, 2), "dev_2": lax.rem(i, 2)}


def outer_peer(o):
    return {"grp": lax.div(o, 4), "dev_0": lax.rem(o, 4)}


def others(me, body):
    def step(k, carry):
        body(k, lax.rem(me + k, 16), lax.rem(me + 16 - k, 16))
        return carry

    lax.fori_loop(1, 16, step, 0)


def greet(inner, outer):
    barrier = pltpu.get_barrier_semaphore()

    def inner_step(k, to, frm):
        pl.semaphore_signal(barrier, inc=1, device_id=inner_peer(to), device_id_type=MESH_IDS)

    def outer_step(k, to, frm):
        pl.semaphore_signal(barrier, inc=1, device_id=outer_peer(to), device_id_type=MESH_IDS)

    others(inner, inner_step)
    others(outer, outer_step)
    return barrier


def send(src, dst, send_sem, recv_sem, peer):
    return pltpu.make_async_remote_copy(
        src_ref=src, dst_ref=dst, send_sem=send_sem, recv_sem=recv_sem, device_id=peer, device_id_type=MESH_IDS
    )


def gather_kernel(sel_ref, place_ref, points_ref, out_ref, rows, line, window, s1, r1, s2, r2, s3, r3):
    inner, outer = position()
    core = lax.rem(inner, 2)
    barrier = greet(inner, outer)
    d = points_ref.shape[1]
    count = points_ref.shape[0]
    pick = (lax.broadcasted_iota(jnp.int32, (SLOTS, count), 1) == sel_ref[...]).astype(BF16)
    picked = jnp.dot(pick, points_ref[...], preferred_element_type=F32).astype(BF16)
    rows[...] = picked
    line[inner] = picked
    pl.semaphore_wait(barrier, 30)

    def first(k, to, frm):
        send(rows, line.at[inner], s1.at[k], r1.at[inner], inner_peer(to)).start()

    others(inner, first)

    def first_done(k, to, frm):
        send(rows, line.at[frm], s1.at[k], r1.at[frm], inner_peer(to)).wait()

    others(inner, first_done)
    pick = (
        lax.broadcasted_iota(jnp.int32, (WINDOW, 16 * SLOTS), 0) == place_ref[...]
    ).astype(BF16)
    compact = jnp.dot(pick, line[...].reshape(16 * SLOTS, d), preferred_element_type=F32).astype(BF16)
    window[...] = compact
    out_ref[outer] = compact
    half = pl.ds(pl.multiple_of(core * (WINDOW // 2), WINDOW // 2), WINDOW // 2)
    rest = pl.ds(pl.multiple_of((1 - core) * (WINDOW // 2), WINDOW // 2), WINDOW // 2)

    def second(k, to, frm):
        send(window.at[half], out_ref.at[outer, half], s2.at[k], r2.at[outer], outer_peer(to)).start()

    others(outer, second)
    partner = {"dev_2": 1 - core}

    def forward(k, to, frm):
        send(window.at[half], out_ref.at[frm, half], s2.at[k], r2.at[frm], outer_peer(to)).wait_recv()
        send(out_ref.at[frm, half], out_ref.at[frm, half], s3.at[k], r3.at[frm], partner).start()

    others(outer, forward)

    def last(k, to, frm):
        send(window.at[half], out_ref.at[frm, half], s2.at[k], r2.at[frm], outer_peer(to)).wait_send()
        copy = send(out_ref.at[frm, rest], out_ref.at[frm, rest], s3.at[k], r3.at[frm], partner)
        copy.wait_send()
        copy.wait_recv()

    others(outer, last)


def gather_windows(sel, place, points):
    d = points.shape[1]
    return pl.pallas_call(
        gather_kernel,
        out_shape=jax.ShapeDtypeStruct((16, WINDOW, d), BF16),
        in_specs=[VMEM, VMEM, VMEM],
        out_specs=VMEM,
        scratch_shapes=[
            pltpu.VMEM((SLOTS, d), BF16),
            pltpu.VMEM((16, SLOTS, d), BF16),
            pltpu.VMEM((WINDOW, d), BF16),
        ]
        + [DMA((16,))] * 6,
        name="gather",
        compiler_params=pltpu.CompilerParams(collective_id=0, has_side_effects=True),
    )(sel, place, points)


def place_kernel(first_ref, windows_ref, before_ref, marks_ref, held):
    n, d = marks_ref.shape
    held[:n, :] = before_ref[...].astype(F32)
    for g in range(16):
        lo = first_ref[g]

        @pl.when(first_ref[g + 1] > lo)
        def _():
            base = pl.multiple_of(lax.div(lo, 8) * 8, 8)
            block = jnp.concatenate([windows_ref[g].astype(F32), jnp.zeros((8, d), F32)], 0)
            moved = pltpu.roll(block, lo - base, 0)
            old = held[pl.ds(base, 8), :]
            at = lax.broadcasted_iota(jnp.int32, (8, d), 0)
            held[pl.ds(base, 8), :] = jnp.where(at >= lo - base, moved[:8], old)
            held[pl.ds(base + 8, WINDOW), :] = moved[8:]

    marks_ref[...] = held[:n, :].astype(BF16)


def place_windows(first, windows, before):
    n, d = before.shape
    return pl.pallas_call(
        place_kernel,
        out_shape=jax.ShapeDtypeStruct((n, d), BF16),
        in_specs=[pl.BlockSpec(memory_space=pltpu.SMEM), VMEM, VMEM],
        out_specs=VMEM,
        scratch_shapes=[pltpu.VMEM((n + WINDOW + 8, d), F32)],
        name="place",
    )(first, windows, before)


def gather_marks(points, ids):
    count, d = points.shape
    n = ids.shape[0]
    devices = lax.axis_size(GRP_DEV)
    me = lax.axis_index(GRP_DEV)
    bounds = jnp.sum(
        (ids[None, :] < (jnp.arange(devices + 1, dtype=jnp.int32) * count)[:, None]).astype(jnp.int32), axis=1
    )
    lines = bounds[::16]
    fits = (jnp.max(bounds[1:] - bounds[:-1]) <= SLOTS) & (jnp.max(lines[1:] - lines[:-1]) <= WINDOW)
    step = jnp.where(fits, n, SLOTS)
    padded = jnp.concatenate([ids, jnp.zeros((SLOTS,), jnp.int32)])
    slot = jnp.arange(SLOTS, dtype=jnp.int32)

    def turn(start, before):
        b = jnp.clip(bounds, start, start + step)
        mine = lax.dynamic_slice(b, (me,), (2,))
        local = lax.dynamic_slice(padded, (mine[0],), (SLOTS,)) - me * count
        sel = jnp.where(mine[0] + slot < mine[1], local, -1)
        line = lax.dynamic_slice(b, (me // 16 * 16,), (17,))
        place = line[:16, None] + slot[None, :]
        place = jnp.where(place < line[1:, None], place - line[0], -1)
        return place_windows(b[::16], gather_windows(sel.reshape(SLOTS, 1), place.reshape(1, 16 * SLOTS), points), before)

    marks = turn(jnp.int32(0), jnp.zeros((n, d), BF16))
    return lax.while_loop(
        lambda c: c[0] < n, lambda c: (c[0] + step, turn(c[0], c[1])), (step, marks)
    )[1]


def stats_kernel(rows_total, stats_ref, out_ref, mid, line, cross, s1, r1, s2, r2):
    inner, outer = position()
    barrier = greet(inner, outer)
    line[inner] = stats_ref[...]
    pl.semaphore_wait(barrier, 30)

    def first(k, to, frm):
        send(stats_ref, line.at[inner], s1.at[k], r1.at[inner], inner_peer(to)).start()

    def first_done(k, to, frm):
        send(stats_ref, line.at[frm], s1.at[k], r1.at[frm], inner_peer(to)).wait()

    others(inner, first)
    others(inner, first_done)
    total = jnp.sum(line[...], axis=0)
    mid[...] = total
    cross[outer] = total

    def second(k, to, frm):
        send(mid, cross.at[outer], s2.at[k], r2.at[outer], outer_peer(to)).start()

    def second_done(k, to, frm):
        send(mid, cross.at[frm], s2.at[k], r2.at[frm], outer_peer(to)).wait()

    others(outer, second)
    others(outer, second_done)
    total = jnp.sum(cross[...], axis=0) / rows_total
    mean = total[:8]
    out_ref[:8] = mean
    out_ref[8:] = lax.rsqrt(jnp.maximum(total[8:] - jnp.square(mean), 0.0) + 1e-05)


def mean_and_scale(stats, rows_total):
    shape = stats.shape
    return pl.pallas_call(
        functools.partial(stats_kernel, rows_total),
        out_shape=jax.ShapeDtypeStruct(shape, F32),
        in_specs=[VMEM],
        out_specs=VMEM,
        scratch_shapes=[
            pltpu.VMEM(shape, F32),
            pltpu.VMEM((16,) + shape, F32),
            pltpu.VMEM((16,) + shape, F32),
        ]
        + [DMA((16,))] * 4,
        name="stats",
        compiler_params=pltpu.CompilerParams(collective_id=1, has_side_effects=True),
    )(stats)


def standardize_kernel(raw_ref, stats_ref, out_ref):
    for i in range(8):
        cols = slice(i * 128, (i + 1) * 128)
        x = raw_ref[:, cols] - stats_ref[i : i + 1, :]
        out_ref[:, cols] = (x * stats_ref[8 + i : 9 + i, :]).astype(BF16)


def standardize(raw, stats):
    rows, n = raw.shape
    block = pl.BlockSpec((ROWS_STEP, n), lambda i: (i, 0))
    return pl.pallas_call(
        standardize_kernel,
        grid=(rows // ROWS_STEP,),
        out_shape=jax.ShapeDtypeStruct((rows, n), BF16),
        in_specs=[block, pl.BlockSpec(stats.shape, lambda i: (0, 0))],
        out_specs=block,
        name="standardize",
    )(raw, stats)


def shards(points, ridge, landmark_ids):
    marks = gather_marks(points, landmark_ids)
    hi, lo, norms = factor(marks, ridge)
    raw, stats = raw_features(points, marks, norms, hi, lo)
    return standardize(raw, mean_and_scale(stats, points.shape[0] * lax.axis_size(GRP_DEV)))


def solution(mesh):
    torus = Mesh(
        mesh.devices.reshape(mesh.shape["grp"], 4, 8, 2), ("grp", "dev_0", "dev_1", "dev_2")
    )
    placed = (P(GRP_DEV, None), P(), P())
    return jax.shard_map(
        shards, mesh=torus, in_specs=placed, out_specs=P(GRP_DEV, None), check_vma=False
    )
```

```python
import functools

import jax
import jax.numpy as jnp
from jax import lax
from jax.experimental import pallas as pl
from jax.experimental.pallas import tpu as pltpu
from jax.sharding import Mesh
from jax.sharding import PartitionSpec as P

GRP_DEV = ("grp", "dev_0", "dev_1", "dev_2")
F32 = jnp.float32
BF16 = jnp.bfloat16
HI = lax.Precision.HIGHEST
BLK = 128
ROWS_STEP = 256
VMEM = pl.BlockSpec(memory_space=pltpu.VMEM)


def lane(x, c):
    return jnp.broadcast_to(x[:, c : c + 1], (8, 128))


def sub(x, k):
    return jnp.broadcast_to(x[k : k + 1, :], (8, 128))


def eliminate64(g1, g2, lane0):
    row = lax.broadcasted_iota(jnp.int32, (8, 128), 0)
    for q in range(8):
        b = [[lane(g1[t], lane0 + 8 * q + c) for t in range(q, 8)] for c in range(8)]
        root = None
        scale, inverse, last_scale, last_inverse = None, None, None, None
        for k in range(8):
            p = sub(b[k][0], k)
            r = 1.0 / p
            rs = lax.rsqrt(p if k == 0 else p * inverse)
            root = rs if k == 0 else jnp.where(row == k, rs, root)
            m = [x * r for x in b[k]]
            m[0] = jnp.where(row > k, m[0], 0.0)
            if k < 7:
                pc, bk = p, b[k]
                if last_inverse is not None:
                    pc, bk = p * last_inverse, [x * last_inverse for x in b[k]]
                for c in range(k + 1, 8):
                    a = sub(b[c][0], k)
                    b[c] = [pc * x - y * a for x, y in zip(b[c], bk)]
                if k == 0:
                    scale, inverse = p, r
                else:
                    next_inverse = inverse * r if last_scale is None else inverse * r * last_scale
                    scale, last_scale = scale * pc, scale
                    inverse, last_inverse = next_inverse, inverse
            a1 = sub(g1[q], k)
            a2 = sub(g2[q], k)
            for t in range(q, 8):
                g1[t] = g1[t] - m[t - q] * a1
                g2[t] = g2[t] - m[t - q] * a2
        g1[q] = g1[q] * root
        g2[q] = g2[q] * root
    return g1, g2


def split(x):
    high = x.astype(BF16)
    return high, (x - high.astype(F32)).astype(BF16)


def cat(xs, axis):
    return jnp.concatenate(xs, axis)


def pair_dot(a, high, low):
    return jnp.dot(a, high, preferred_element_type=F32) + jnp.dot(a, low, preferred_element_type=F32)


def inverse_factor(s, eye):
    rows = lambda x: [x[8 * t : 8 * t + 8] for t in range(8)]
    u, v = eliminate64(rows(s[:64]), rows(eye[:64]), 0)
    v = cat(v, 0)
    high, low = split(cat([cat(u, 0), v], 1))
    uh, ul = high[:, :BLK], low[:, :BLK]
    t = lax.dot_general(
        cat([uh, ul, uh, ul], 0),
        cat([high, high, low, low], 0),
        (((0,), (0,)), ((), ())),
        preferred_element_type=F32,
    )[64:]
    _, v2 = eliminate64(rows(s[64:] - t[:, :BLK]), rows(eye[64:] - t[:, BLK:]), 64)
    return cat([v] + v2, 0)


def factor_kernel(marks_ref, ridge_ref, hi_ref, lo_ref, norm_ref, m, rt, rh, rl):
    n, d = marks_ref.shape
    nb = n // BLK
    eye = (
        lax.broadcasted_iota(jnp.int32, (BLK, BLK), 0)
        == lax.broadcasted_iota(jnp.int32, (BLK, BLK), 1)
    ).astype(F32)
    sq = jnp.square(marks_ref[...].astype(F32))
    nr = lax.dot_general(
        jnp.ones((8, d), F32), sq, (((1,), (1,)), ((), ())), preferred_element_type=F32, precision=HI
    )
    norm_ref[...] = nr
    for i in range(nb):
        rows = slice(i * BLK, (i + 1) * BLK)
        blk = marks_ref[rows, :]
        nc = jnp.sum(jnp.square(blk.astype(F32)), axis=1, keepdims=True)
        g = lax.dot_general(blk, marks_ref[...], (((1,), (1,)), ((), ())), preferred_element_type=F32)
        m[rows, :] = jnp.exp((2.0 * g - nc - nr[:1]) * (1.0 / (2.0 * d)))
        m[rows, rows] += eye * ridge_ref[:, rows]
    rt[...] = jnp.zeros_like(rt)
    rh[...] = jnp.zeros_like(rh)
    rl[...] = jnp.zeros_like(rl)

    def step(j, carry):
        here = pl.ds(pl.multiple_of(j * BLK, BLK), BLK)
        linv = inverse_factor(m[here, here], eye)
        for i in range(1, nb):
            rows = slice(i * BLK, (i + 1) * BLK)
            m[rows, :] = m[rows, :] - pair_dot(rt[rows, :], rh[...], rl[...])
        m[here, here] = eye
        high, low = split(m[here, :])
        r = pair_dot(cat(split(linv), 1), cat([high, high], 0), cat([low, low], 0))
        m[here, :] = r
        high, low = split(r)
        rh[:BLK, :] = high
        rh[BLK:, :] = high
        rl[:BLK, :] = low
        rl[BLK:, :] = low
        for i in range(1, nb):
            rows = slice(i * BLK, (i + 1) * BLK)
            m[rows, here] = jnp.where(i > j, 0.0, m[rows, here])
            high, low = split(jnp.where(i > j + 1, r[:, rows].T, 0.0))
            rt[rows, :BLK] = high
            rt[rows, BLK:] = low
        after = pl.ds(pl.multiple_of(jnp.minimum(j + 1, nb - 1) * BLK, BLK), BLK)
        t = jnp.where(j + 1 < nb, m[here, after].T, 0.0)
        m[after, :] = m[after, :] - pair_dot(cat(split(t), 1), rh[...], rl[...])
        return carry

    lax.fori_loop(0, nb, step, 0)
    for i in range(nb):
        rows = slice(i * BLK, (i + 1) * BLK)
        x = m[rows, :]
        x = jnp.where(lax.broadcasted_iota(jnp.int32, x.shape, 1) < (i + 1) * BLK, x, 0.0)
        hi_ref[rows, :], lo_ref[rows, :] = split(x)


def factor(marks, ridge):
    n = marks.shape[0]
    return pl.pallas_call(
        factor_kernel,
        out_shape=[
            jax.ShapeDtypeStruct((n, n), BF16),
            jax.ShapeDtypeStruct((n, n), BF16),
            jax.ShapeDtypeStruct((8, n), F32),
        ],
        in_specs=[VMEM, VMEM],
        out_specs=[VMEM, VMEM, VMEM],
        scratch_shapes=[
            pltpu.VMEM((n, n), F32),
            pltpu.VMEM((n, 2 * BLK), BF16),
            pltpu.VMEM((2 * BLK, n), BF16),
            pltpu.VMEM((2 * BLK, n), BF16),
        ],
        name="factor",
        compiler_params=pltpu.CompilerParams(vmem_limit_bytes=40 << 20),
    )(marks, ridge.reshape(1, n))


MESH_IDS = pl.DeviceIdType.MESH
SLOTS = 16
WINDOW = 128
DMA = pltpu.SemaphoreType.DMA


def position():
    inner = lax.axis_index("dev_1") * 2 + lax.axis_index("dev_2")
    outer = lax.axis_index("grp") * 4 + lax.axis_index("dev_0")
    return inner, outer


def inner_peer(i):
    return {"dev_1": lax.div(i, 2), "dev_2": lax.rem(i, 2)}


def outer_peer(o):
    return {"grp": lax.div(o, 4), "dev_0": lax.rem(o, 4)}


def others(me, body):
    def step(k, carry):
        body(k, lax.rem(me + k, 16), lax.rem(me + 16 - k, 16))
        return carry

    lax.fori_loop(1, 16, step, 0)


def greet(inner, outer):
    barrier = pltpu.get_barrier_semaphore()

    def inner_step(k, to, frm):
        pl.semaphore_signal(barrier, inc=1, device_id=inner_peer(to), device_id_type=MESH_IDS)

    def outer_step(k, to, frm):
        pl.semaphore_signal(barrier, inc=1, device_id=outer_peer(to), device_id_type=MESH_IDS)

    others(inner, inner_step)
    others(outer, outer_step)
    return barrier


def send(src, dst, send_sem, recv_sem, peer):
    return pltpu.make_async_remote_copy(
        src_ref=src, dst_ref=dst, send_sem=send_sem, recv_sem=recv_sem, device_id=peer, device_id_type=MESH_IDS
    )


def count_below(ids, starts):
    return jnp.sum((ids < starts).astype(F32), axis=1, keepdims=True).astype(jnp.int32)


def gather_kernel(
    ids_ref, turn_ref, points_ref, marks_ref, over_ref, rows, line, window, windows, s1, r1, s2, r2, s3, r3
):
    inner, outer = position()
    core = lax.rem(inner, 2)
    barrier = greet(inner, outer)
    count, d = points_ref.shape
    n = marks_ref.shape[0]
    iota = lambda shape, axis: lax.broadcasted_iota(jnp.int32, shape, axis)
    ids = ids_ref[...]
    low, high = turn_ref[0:1, 0:1], turn_ref[1:2, 0:1]
    clip = lambda x: jnp.minimum(jnp.maximum(x, low), high)
    start = (outer * 16 + inner) * count
    first = clip(count_below(ids, jnp.full((1, n), start)))
    mark = iota((SLOTS, n), 1)
    wanted = (
        (mark - first == iota((SLOTS, n), 0)) & (ids >= start) & (ids < start + count) & (mark < high)
    )
    sel = jnp.sum(jnp.where(wanted, ids - start + 1, 0).astype(F32), axis=1, keepdims=True) - 1.0
    pick = (iota((SLOTS, count), 1).astype(F32) == sel).astype(BF16)
    picked = jnp.dot(pick, points_ref[...], preferred_element_type=F32).astype(BF16)
    rows[...] = picked
    line[inner] = picked
    at = clip(count_below(ids, (outer * 16 + iota((24, n), 0)) * count))
    slot = iota((1, 16 * SLOTS), 1)
    place, limit = slot, slot
    for i in range(16):
        own = (slot >= i * SLOTS) & (slot < (i + 1) * SLOTS)
        place = jnp.where(own, at[i : i + 1] + (slot - i * SLOTS), place)
        limit = jnp.where(own, at[i + 1 : i + 2], limit)
    place = jnp.where(place < limit, place - at[0:1], -1)
    pick = (iota((WINDOW, 16 * SLOTS), 0) == place).astype(BF16)
    lines = count_below(ids, iota((24, n), 0) * (16 * count))
    owned = jnp.zeros((256, 1), F32)
    for i in range(n // 128):
        part = ids[:, i * 128 : (i + 1) * 128]
        begin = iota((256, 128), 0) * count
        hit = ((part >= begin) & (part < begin + count)).astype(F32)
        owned = owned + hit
    owned = jnp.max(jnp.sum(owned, axis=1, keepdims=True), axis=0, keepdims=True)
    longest = jnp.max(lines[1:17] - lines[0:16], axis=0, keepdims=True)
    over = (owned > SLOTS) | (longest > WINDOW)
    over_ref[...] = jnp.broadcast_to(over.astype(jnp.int32), over_ref.shape)
    lines = clip(lines)
    pl.semaphore_wait(barrier, 30)

    def first_send(k, to, frm):
        send(rows, line.at[inner], s1.at[k], r1.at[inner], inner_peer(to)).start()

    def first_done(k, to, frm):
        send(rows, line.at[frm], s1.at[k], r1.at[frm], inner_peer(to)).wait()

    others(inner, first_send)
    others(inner, first_done)
    compact = jnp.dot(pick, line[...].reshape(16 * SLOTS, d), preferred_element_type=F32).astype(BF16)
    window[...] = compact
    windows[outer] = compact
    half = pl.ds(pl.multiple_of(core * (WINDOW // 2), WINDOW // 2), WINDOW // 2)
    rest = pl.ds(pl.multiple_of((1 - core) * (WINDOW // 2), WINDOW // 2), WINDOW // 2)

    def second(k, to, frm):
        send(window.at[half], windows.at[outer, half], s2.at[k], r2.at[outer], outer_peer(to)).start()

    others(outer, second)
    partner = {"dev_2": 1 - core}

    def forward(k, to, frm):
        send(window.at[half], windows.at[frm, half], s2.at[k], r2.at[frm], outer_peer(to)).wait_recv()
        send(windows.at[frm, half], windows.at[frm, half], s3.at[k], r3.at[frm], partner).start()

    others(outer, forward)

    def last(k, to, frm):
        send(window.at[half], windows.at[frm, half], s2.at[k], r2.at[frm], outer_peer(to)).wait_send()
        copy = send(windows.at[frm, rest], windows.at[frm, rest], s3.at[k], r3.at[frm], partner)
        copy.wait_send()
        copy.wait_recv()

    others(outer, last)
    slot = iota((1, WINDOW), 1)
    places = []
    for g in range(16):
        place = lines[g : g + 1] + slot
        places.append(jnp.where(place < lines[g + 1 : g + 2], place, -1))
    source = windows[...].reshape(16 * WINDOW, d)
    for i in range(n // 128):
        row = iota((128, WINDOW), 0) + i * 128
        hot = cat([(row == place).astype(BF16) for place in places], 1)
        marks_ref[i * 128 : (i + 1) * 128, :] = jnp.dot(hot, source, preferred_element_type=F32).astype(BF16)


def gather_turn(ids, turn, points):
    d = points.shape[1]
    n = ids.shape[1]
    return pl.pallas_call(
        gather_kernel,
        out_shape=[jax.ShapeDtypeStruct((n, d), BF16), jax.ShapeDtypeStruct((8, 128), jnp.int32)],
        in_specs=[VMEM, VMEM, VMEM],
        out_specs=[VMEM, VMEM],
        scratch_shapes=[
            pltpu.VMEM((SLOTS, d), BF16),
            pltpu.VMEM((16, SLOTS, d), BF16),
            pltpu.VMEM((WINDOW, d), BF16),
            pltpu.VMEM((16, WINDOW, d), BF16),
        ]
        + [DMA((16,))] * 6,
        name="gather",
        compiler_params=pltpu.CompilerParams(
            collective_id=0, has_side_effects=True, vmem_limit_bytes=16 << 20
        ),
    )(ids, turn, points)


def gather_marks(points, ids):
    n = ids.shape[0]
    ids = ids.reshape(1, n)
    place = jnp.arange(n, dtype=jnp.int32)[:, None]

    def turn(low, high):
        bounds = jnp.stack([low, high]).astype(jnp.int32)
        return gather_turn(ids, jnp.broadcast_to(bounds[:, None], (2, 128)), points)

    marks, over = turn(jnp.int32(0), jnp.int32(n))

    def again(state):
        low, marks = state
        fresh = turn(low, low + SLOTS)[0]
        return low + SLOTS, jnp.where((place >= low) & (place < low + SLOTS), fresh, marks)

    return lax.while_loop(lambda s: s[0] < n, again, (jnp.where(over[0, 0] > 0, 0, n), marks))[1]


def raw_kernel(
    rows_total, points_ref, marks_ref, norm_ref, hi_ref, lo_ref, raw_ref, out_ref, own, mid, line, cross, s1, r1, s2, r2
):
    inner, outer = position()
    barrier = greet(inner, outer)
    rows, d = points_ref.shape
    n = marks_ref.shape[0]
    own[...] = jnp.zeros_like(own)

    def block(i, carry):
        here = pl.ds(pl.multiple_of(i * ROWS_STEP, ROWS_STEP), ROWS_STEP)
        pts = points_ref[here, :]
        nc = jnp.sum(jnp.square(pts.astype(F32)), axis=1, keepdims=True)
        g = lax.dot_general(pts, marks_ref[...], (((1,), (1,)), ((), ())), preferred_element_type=F32)
        ch, cl = split(jnp.exp((2.0 * g - nc - norm_ref[:1, :]) * (1.0 / (2.0 * d))))
        for j in range(n // 256):
            cols = slice(j * 256, (j + 1) * 256)
            k = (j + 1) * 256
            mul = lambda a, b: lax.dot_general(
                a, b, (((1,), (1,)), ((), ())), preferred_element_type=F32
            )
            x = mul(ch[:, :k], hi_ref[cols, :k])
            x += mul(cl[:, :k], hi_ref[cols, :k])
            x += mul(ch[:, :k], lo_ref[cols, :k])
            raw_ref[here, cols] = x
            for h in range(2):
                y = x[:, h * 128 : (h + 1) * 128]
                r = 2 * j + h
                own[r : r + 1, :] += jnp.sum(y, axis=0, keepdims=True)
                own[8 + r : 9 + r, :] += jnp.sum(jnp.square(y), axis=0, keepdims=True)
        return carry

    lax.fori_loop(0, rows // ROWS_STEP, block, 0)
    line[inner] = own[...]
    pl.semaphore_wait(barrier, 30)

    def first(k, to, frm):
        send(own, line.at[inner], s1.at[k], r1.at[inner], inner_peer(to)).start()

    def first_done(k, to, frm):
        send(own, line.at[frm], s1.at[k], r1.at[frm], inner_peer(to)).wait()

    others(inner, first)
    others(inner, first_done)
    total = jnp.sum(line[...], axis=0)
    mid[...] = total
    cross[outer] = total

    def second(k, to, frm):
        send(mid, cross.at[outer], s2.at[k], r2.at[outer], outer_peer(to)).start()

    def second_done(k, to, frm):
        send(mid, cross.at[frm], s2.at[k], r2.at[frm], outer_peer(to)).wait()

    others(outer, second)
    others(outer, second_done)
    total = jnp.sum(cross[...], axis=0) / rows_total
    mean = total[:8]
    out_ref[:8] = mean
    out_ref[8:] = lax.rsqrt(jnp.maximum(total[8:] - jnp.square(mean), 0.0) + 1e-05)


def raw_features(points, marks, norms, hi, lo, rows_total):
    rows = points.shape[0]
    n = marks.shape[0]
    shape = (16, n // 8)
    return pl.pallas_call(
        functools.partial(raw_kernel, rows_total),
        out_shape=[jax.ShapeDtypeStruct((rows, n), F32), jax.ShapeDtypeStruct(shape, F32)],
        in_specs=[VMEM] * 5,
        out_specs=[VMEM, VMEM],
        scratch_shapes=[
            pltpu.VMEM(shape, F32),
            pltpu.VMEM(shape, F32),
            pltpu.VMEM((16,) + shape, F32),
            pltpu.VMEM((16,) + shape, F32),
        ]
        + [DMA((16,))] * 4,
        name="raw",
        compiler_params=pltpu.CompilerParams(
            collective_id=1, has_side_effects=True, vmem_limit_bytes=40 << 20
        ),
    )(points, marks, norms, hi, lo)


def standardize_kernel(raw_ref, stats_ref, out_ref, buf, sems):
    steps = raw_ref.shape[0] // ROWS_STEP
    copies = []
    for s in range(steps):
        rows = slice(s * ROWS_STEP, (s + 1) * ROWS_STEP)
        if s >= 2:
            copies[s - 2].wait()
        for i in range(8):
            cols = slice(i * 128, (i + 1) * 128)
            x = raw_ref[rows, cols] - stats_ref[i : i + 1, :]
            buf[s % 2, :, cols] = (x * stats_ref[8 + i : 9 + i, :]).astype(BF16)
        copies.append(pltpu.make_async_copy(buf.at[s % 2], out_ref.at[rows, :], sems.at[s % 2]))
        copies[s].start()
    copies[steps - 2].wait()
    copies[steps - 1].wait()


def standardize(raw, stats):
    rows, n = raw.shape
    return pl.pallas_call(
        standardize_kernel,
        out_shape=jax.ShapeDtypeStruct((rows, n), BF16),
        in_specs=[VMEM, VMEM],
        out_specs=pl.BlockSpec(memory_space=pl.ANY),
        scratch_shapes=[pltpu.VMEM((2, ROWS_STEP, n), BF16), DMA((2,))],
        name="standardize",
        compiler_params=pltpu.CompilerParams(vmem_limit_bytes=16 << 20),
    )(raw, stats)


def shards(points, ridge, landmark_ids):
    marks = gather_marks(points, landmark_ids)
    hi, lo, norms = factor(marks, ridge)
    raw, stats = raw_features(points, marks, norms, hi, lo, points.shape[0] * lax.axis_size(GRP_DEV))
    return standardize(raw, stats)


def solution(mesh):
    torus = Mesh(
        mesh.devices.reshape(mesh.shape["grp"], 4, 8, 2), ("grp", "dev_0", "dev_1", "dev_2")
    )
    placed = (P(GRP_DEV, None), P(), P())
    return jax.shard_map(
        shards, mesh=torus, in_specs=placed, out_specs=P(GRP_DEV, None), check_vma=False
    )
```

```python
import functools

import jax
import jax.numpy as jnp
from jax import lax
from jax.experimental import pallas as pl
from jax.experimental.pallas import tpu as pltpu
from jax.sharding import Mesh
from jax.sharding import PartitionSpec as P

GRP_DEV = ("grp", "dev_0", "dev_1", "dev_2")
F32 = jnp.float32
BF16 = jnp.bfloat16
HI = lax.Precision.HIGHEST
BLK = 128
ROWS_STEP = 256
VMEM = pl.BlockSpec(memory_space=pltpu.VMEM)


def lane(x, c):
    return jnp.broadcast_to(x[:, c : c + 1], (8, 128))


def sub(x, k):
    return jnp.broadcast_to(x[k : k + 1, :], (8, 128))


def eliminate64(g1, g2, lane0):
    row = lax.broadcasted_iota(jnp.int32, (8, 128), 0)
    for q in range(8):
        b = [[lane(g1[t], lane0 + 8 * q + c) for t in range(q, 8)] for c in range(8)]
        root = None
        scale, inverse, last_scale, last_inverse = None, None, None, None
        for k in range(8):
            p = sub(b[k][0], k)
            r = 1.0 / p
            rs = lax.rsqrt(p if k == 0 else p * inverse)
            root = rs if k == 0 else jnp.where(row == k, rs, root)
            m = [x * r for x in b[k]]
            m[0] = jnp.where(row > k, m[0], 0.0)
            if k < 7:
                pc, bk = p, b[k]
                if last_inverse is not None:
                    pc, bk = p * last_inverse, [x * last_inverse for x in b[k]]
                for c in range(k + 1, 8):
                    a = sub(b[c][0], k)
                    b[c] = [pc * x - y * a for x, y in zip(b[c], bk)]
                if k == 0:
                    scale, inverse = p, r
                else:
                    next_inverse = inverse * r if last_scale is None else inverse * r * last_scale
                    scale, last_scale = scale * pc, scale
                    inverse, last_inverse = next_inverse, inverse
            a1 = sub(g1[q], k)
            a2 = sub(g2[q], k)
            for t in range(q, 8):
                g1[t] = g1[t] - m[t - q] * a1
                g2[t] = g2[t] - m[t - q] * a2
        g1[q] = g1[q] * root
        g2[q] = g2[q] * root
    return g1, g2


def split(x):
    high = x.astype(BF16)
    return high, (x - high.astype(F32)).astype(BF16)


def cat(xs, axis):
    return jnp.concatenate(xs, axis)


def pair_dot(a, high, low):
    return jnp.dot(a, high, preferred_element_type=F32) + jnp.dot(a, low, preferred_element_type=F32)


def inverse_factor(s, eye):
    rows = lambda x: [x[8 * t : 8 * t + 8] for t in range(8)]
    u, v = eliminate64(rows(s[:64]), rows(eye[:64]), 0)
    v = cat(v, 0)
    high, low = split(cat([cat(u, 0), v], 1))
    uh, ul = high[:, :BLK], low[:, :BLK]
    t = lax.dot_general(
        cat([uh, ul, uh, ul], 0),
        cat([high, high, low, low], 0),
        (((0,), (0,)), ((), ())),
        preferred_element_type=F32,
    )[64:]
    _, v2 = eliminate64(rows(s[64:] - t[:, :BLK]), rows(eye[64:] - t[:, BLK:]), 64)
    return cat([v] + v2, 0)


def factor_kernel(marks_ref, ridge_ref, hi_ref, lo_ref, norm_ref, m, diag, inv, rt, rh, rl):
    n, d = marks_ref.shape
    nb = n // BLK
    eye = (
        lax.broadcasted_iota(jnp.int32, (BLK, BLK), 0)
        == lax.broadcasted_iota(jnp.int32, (BLK, BLK), 1)
    ).astype(F32)
    column = lax.broadcasted_iota(jnp.int32, (BLK, n), 1)
    sq = jnp.square(marks_ref[...].astype(F32))
    nr = lax.dot_general(
        jnp.ones((8, d), F32), sq, (((1,), (1,)), ((), ())), preferred_element_type=F32, precision=HI
    )
    norm_ref[...] = nr

    def core_rows(i):
        rows = slice(i * BLK, (i + 1) * BLK)
        blk = marks_ref[rows, :]
        nc = jnp.sum(jnp.square(blk.astype(F32)), axis=1, keepdims=True)
        g = lax.dot_general(blk, marks_ref[...], (((1,), (1,)), ((), ())), preferred_element_type=F32)
        m[rows, :] = jnp.exp((2.0 * g - nc - nr[:1]) * (1.0 / (2.0 * d)))
        m[rows, rows] += eye * ridge_ref[:, rows]

    def finish_row(j):
        here = pl.ds(pl.multiple_of(j * BLK, BLK), BLK)
        m[here, here] = eye
        high, low = split(m[here, :])
        r = pair_dot(cat(split(inv[...]), 1), cat([high, high], 0), cat([low, low], 0))
        high, low = split(r)
        keep = column < (j + 1) * BLK
        hi_ref[here, :] = jnp.where(keep, high, jnp.zeros_like(high))
        lo_ref[here, :] = jnp.where(keep, low, jnp.zeros_like(low))
        return r, high, low

    def update_rows(j):
        here = pl.ds(pl.multiple_of(j * BLK, BLK), BLK)
        r, high, low = finish_row(j)
        rh[:BLK, :] = high
        rh[BLK:, :] = high
        rl[:BLK, :] = low
        rl[BLK:, :] = low
        for i in range(1, nb):
            rows = slice(i * BLK, (i + 1) * BLK)
            m[rows, here] = jnp.where(i > j, 0.0, m[rows, here])
            high, low = split(jnp.where(i > j, r[:, rows].T, 0.0))
            rt[rows, :BLK] = high
            rt[rows, BLK:] = low
        for i in range(1, nb):
            rows = slice(i * BLK, (i + 1) * BLK)
            m[rows, :] = m[rows, :] - pair_dot(rt[rows, :], rh[...], rl[...])

    def next_diagonal(j, linv):
        here = pl.ds(pl.multiple_of(j * BLK, BLK), BLK)
        after = pl.ds(pl.multiple_of(jnp.minimum(j + 1, nb - 1) * BLK, BLK), BLK)
        high, low = split(m[here, after])
        u = pair_dot(cat(split(linv), 1), cat([high, high], 0), cat([low, low], 0))
        high, low = split(u)
        t = u.T
        diag[...] = m[after, after] - pair_dot(
            cat(split(t), 1), cat([high, high], 0), cat([low, low], 0)
        )
        inv[...] = linv

    core_rows(0)
    linv = inverse_factor(m[:BLK, :BLK], eye)
    for i in range(1, nb):
        core_rows(i)
    next_diagonal(0, linv)

    def step(j, carry):
        linv = inverse_factor(diag[...], eye)
        update_rows(j - 1)
        next_diagonal(j, linv)
        return carry

    lax.fori_loop(1, nb, step, 0)
    finish_row(nb - 1)


def factor(marks, ridge):
    n = marks.shape[0]
    return pl.pallas_call(
        factor_kernel,
        out_shape=[
            jax.ShapeDtypeStruct((n, n), BF16),
            jax.ShapeDtypeStruct((n, n), BF16),
            jax.ShapeDtypeStruct((8, n), F32),
        ],
        in_specs=[VMEM, VMEM],
        out_specs=[VMEM, VMEM, VMEM],
        scratch_shapes=[
            pltpu.VMEM((n, n), F32),
            pltpu.VMEM((BLK, BLK), F32),
            pltpu.VMEM((BLK, BLK), F32),
            pltpu.VMEM((n, 2 * BLK), BF16),
            pltpu.VMEM((2 * BLK, n), BF16),
            pltpu.VMEM((2 * BLK, n), BF16),
        ],
        name="factor",
        compiler_params=pltpu.CompilerParams(vmem_limit_bytes=40 << 20),
    )(marks, ridge.reshape(1, n))


MESH_IDS = pl.DeviceIdType.MESH
SLOTS = 16
WINDOW = 128
DMA = pltpu.SemaphoreType.DMA


def position():
    inner = lax.axis_index("dev_1") * 2 + lax.axis_index("dev_2")
    outer = lax.axis_index("grp") * 4 + lax.axis_index("dev_0")
    return inner, outer


def inner_peer(i):
    return {"dev_1": lax.div(i, 2), "dev_2": lax.rem(i, 2)}


def outer_peer(o):
    return {"grp": lax.div(o, 4), "dev_0": lax.rem(o, 4)}


def others(me, body):
    def step(k, carry):
        body(k, lax.rem(me + k, 16), lax.rem(me + 16 - k, 16))
        return carry

    lax.fori_loop(1, 16, step, 0)


def greet(inner, outer):
    barrier = pltpu.get_barrier_semaphore()

    def inner_step(k, to, frm):
        pl.semaphore_signal(barrier, inc=1, device_id=inner_peer(to), device_id_type=MESH_IDS)

    def outer_step(k, to, frm):
        pl.semaphore_signal(barrier, inc=1, device_id=outer_peer(to), device_id_type=MESH_IDS)

    others(inner, inner_step)
    others(outer, outer_step)
    return barrier


def send(src, dst, send_sem, recv_sem, peer):
    return pltpu.make_async_remote_copy(
        src_ref=src, dst_ref=dst, send_sem=send_sem, recv_sem=recv_sem, device_id=peer, device_id_type=MESH_IDS
    )


def count_below(ids, starts):
    return jnp.sum((ids < starts).astype(F32), axis=1, keepdims=True).astype(jnp.int32)


def gather_kernel(
    ids_ref, turn_ref, points_ref, marks_ref, over_ref, rows, line, window, windows, hot, s1, r1, s2, r2, s3, r3
):
    inner, outer = position()
    core = lax.rem(inner, 2)
    barrier = greet(inner, outer)
    count, d = points_ref.shape
    n = marks_ref.shape[0]
    iota = lambda shape, axis: lax.broadcasted_iota(jnp.int32, shape, axis)
    ids = ids_ref[...]
    low, high = turn_ref[0:1, 0:1], turn_ref[1:2, 0:1]
    clip = lambda x: jnp.minimum(jnp.maximum(x, low), high)
    start = (outer * 16 + inner) * count
    first = clip(count_below(ids, jnp.full((1, n), start)))
    mark = iota((SLOTS, n), 1)
    wanted = (
        (mark - first == iota((SLOTS, n), 0)) & (ids >= start) & (ids < start + count) & (mark < high)
    )
    sel = jnp.sum(jnp.where(wanted, ids - start + 1, 0).astype(F32), axis=1, keepdims=True) - 1.0
    pick = (iota((SLOTS, count), 1).astype(F32) == sel).astype(BF16)
    picked = jnp.dot(pick, points_ref[...], preferred_element_type=F32).astype(BF16)
    rows[0] = picked[:, :128]
    rows[1] = picked[:, 128:]
    line[inner] = rows[core]
    at = clip(count_below(ids, (outer * 16 + iota((24, n), 0)) * count))
    slot = iota((1, 16 * SLOTS), 1)
    place, limit = slot, slot
    for i in range(16):
        own = (slot >= i * SLOTS) & (slot < (i + 1) * SLOTS)
        place = jnp.where(own, at[i : i + 1] + (slot - i * SLOTS), place)
        limit = jnp.where(own, at[i + 1 : i + 2], limit)
    place = jnp.where(place < limit, place - at[0:1], -1)
    pick = (iota((WINDOW, 16 * SLOTS), 0) == place).astype(BF16)
    lines = count_below(ids, iota((24, n), 0) * (16 * count))
    owned = jnp.zeros((256, 1), F32)
    for i in range(n // 128):
        part = ids[:, i * 128 : (i + 1) * 128]
        begin = iota((256, 128), 0) * count
        hit = ((part >= begin) & (part < begin + count)).astype(F32)
        owned = owned + hit
    owned = jnp.max(jnp.sum(owned, axis=1, keepdims=True), axis=0, keepdims=True)
    longest = jnp.max(lines[1:17] - lines[0:16], axis=0, keepdims=True)
    over = (owned > SLOTS) | (longest > WINDOW)
    over_ref[...] = jnp.broadcast_to(over.astype(jnp.int32), over_ref.shape)
    lines = clip(lines)
    pl.semaphore_wait(barrier, 30)

    def first_send(k, to, frm):
        send(rows.at[lax.rem(to, 2)], line.at[inner], s1.at[k], r1.at[inner], inner_peer(to)).start()

    def first_done(k, to, frm):
        send(rows.at[lax.rem(to, 2)], line.at[frm], s1.at[k], r1.at[frm], inner_peer(to)).wait()

    others(inner, first_send)
    slot = iota((1, WINDOW), 1)
    places = []
    for g in range(16):
        place = lines[g : g + 1] + slot
        places.append(jnp.where(place < lines[g + 1 : g + 2], place, -1))
    for i in range(n // 128):
        row = iota((128, WINDOW), 0) + i * 128
        hot[i * 128 : (i + 1) * 128, :] = cat([(row == place).astype(BF16) for place in places], 1)
    others(inner, first_done)
    compact = jnp.dot(pick, line[...].reshape(16 * SLOTS, 128), preferred_element_type=F32).astype(BF16)
    window[...] = compact
    windows[core, outer] = compact
    partner = {"dev_2": 1 - core}

    def second(k, to, frm):
        send(window, windows.at[core, outer], s2.at[k], r2.at[outer], outer_peer(to)).start()

    others(outer, second)
    send(window, windows.at[core, outer], s3.at[0], r3.at[outer], partner).start()

    def forward(k, to, frm):
        send(window, windows.at[core, frm], s2.at[k], r2.at[frm], outer_peer(to)).wait_recv()
        send(windows.at[core, frm], windows.at[core, frm], s3.at[k], r3.at[frm], partner).start()

    others(outer, forward)

    def last(k, to, frm):
        send(window, windows.at[core, frm], s2.at[k], r2.at[frm], outer_peer(to)).wait_send()
        copy = send(windows.at[1 - core, frm], windows.at[1 - core, frm], s3.at[k], r3.at[frm], partner)
        copy.wait_send()
        copy.wait_recv()

    copy = send(window, windows.at[1 - core, outer], s3.at[0], r3.at[outer], partner)
    copy.wait_send()
    copy.wait_recv()
    others(outer, last)
    source = cat([windows[0].reshape(16 * WINDOW, 128), windows[1].reshape(16 * WINDOW, 128)], 1)
    for i in range(n // 256):
        part = slice(i * 256, (i + 1) * 256)
        marks_ref[part, :] = jnp.dot(hot[part, :], source, preferred_element_type=F32).astype(BF16)


def gather_turn(ids, turn, points):
    d = points.shape[1]
    n = ids.shape[1]
    return pl.pallas_call(
        gather_kernel,
        out_shape=[jax.ShapeDtypeStruct((n, d), BF16), jax.ShapeDtypeStruct((8, 128), jnp.int32)],
        in_specs=[VMEM, VMEM, VMEM],
        out_specs=[VMEM, VMEM],
        scratch_shapes=[
            pltpu.VMEM((2, SLOTS, d // 2), BF16),
            pltpu.VMEM((16, SLOTS, d // 2), BF16),
            pltpu.VMEM((WINDOW, d // 2), BF16),
            pltpu.VMEM((2, 16, WINDOW, d // 2), BF16),
            pltpu.VMEM((n, 16 * WINDOW), BF16),
        ]
        + [DMA((16,))] * 6,
        name="gather",
        compiler_params=pltpu.CompilerParams(
            collective_id=0, has_side_effects=True, vmem_limit_bytes=24 << 20
        ),
    )(ids, turn, points)


def gather_marks(points, ids):
    n = ids.shape[0]
    ids = ids.reshape(1, n)
    place = jnp.arange(n, dtype=jnp.int32)[:, None]

    def turn(low, high):
        bounds = jnp.stack([low, high]).astype(jnp.int32)
        return gather_turn(ids, jnp.broadcast_to(bounds[:, None], (2, 128)), points)

    marks, over = turn(jnp.int32(0), jnp.int32(n))

    def again(state):
        low, marks = state
        fresh = turn(low, low + SLOTS)[0]
        return low + SLOTS, jnp.where((place >= low) & (place < low + SLOTS), fresh, marks)

    return lax.while_loop(lambda s: s[0] < n, again, (jnp.where(over[0, 0] > 0, 0, n), marks))[1]


def raw_kernel(
    rows_total, points_ref, marks_ref, norm_ref, hi_ref, lo_ref, raw_ref, out_ref, own, mid, line, cross, s1, r1, s2, r2
):
    inner, outer = position()
    core = lax.rem(inner, 2)
    barrier = greet(inner, outer)
    cross_peer = lambda o, c: {"grp": lax.div(o, 4), "dev_0": lax.rem(o, 4), "dev_2": c}

    def greet_cross(k, to, frm):
        pl.semaphore_signal(barrier, inc=1, device_id=cross_peer(to, 1 - core), device_id_type=MESH_IDS)

    others(outer, greet_cross)
    rows, d = points_ref.shape
    n = marks_ref.shape[0]
    own[...] = jnp.zeros_like(own)

    def block(i, carry):
        here = pl.ds(pl.multiple_of(i * ROWS_STEP, ROWS_STEP), ROWS_STEP)
        pts = points_ref[here, :]
        nc = jnp.sum(jnp.square(pts.astype(F32)), axis=1, keepdims=True)
        g = lax.dot_general(pts, marks_ref[...], (((1,), (1,)), ((), ())), preferred_element_type=F32)
        ch, cl = split(jnp.exp((2.0 * g - nc - norm_ref[:1, :]) * (1.0 / (2.0 * d))))
        for j in range(n // 256):
            cols = slice(j * 256, (j + 1) * 256)
            k = (j + 1) * 256
            mul = lambda a, b: lax.dot_general(
                a, b, (((1,), (1,)), ((), ())), preferred_element_type=F32
            )
            x = mul(ch[:, :k], hi_ref[cols, :k])
            x += mul(cl[:, :k], hi_ref[cols, :k])
            x += mul(ch[:, :k], lo_ref[cols, :k])
            raw_ref[here, cols] = x
            for h in range(2):
                y = x[:, h * 128 : (h + 1) * 128]
                r = 2 * j + h
                own[0, r : r + 1, :] += jnp.sum(y, axis=0, keepdims=True)
                own[1, r : r + 1, :] += jnp.sum(jnp.square(y), axis=0, keepdims=True)
        return carry

    lax.fori_loop(0, rows // ROWS_STEP, block, 0)
    line[inner] = own[core]
    pl.semaphore_wait(barrier, 45)

    def first(k, to, frm):
        send(own.at[lax.rem(to, 2)], line.at[inner], s1.at[k], r1.at[inner], inner_peer(to)).start()

    def first_done(k, to, frm):
        send(own.at[lax.rem(to, 2)], line.at[frm], s1.at[k], r1.at[frm], inner_peer(to)).wait()

    others(inner, first)
    others(inner, first_done)
    total = jnp.sum(line[...], axis=0)
    mid[...] = total
    cross[core, outer] = total
    partner = {"dev_2": 1 - core}

    def second(k, to, frm):
        for c in (core, 1 - core):
            send(mid, cross.at[core, outer], s2.at[c, k], r2.at[core, outer], cross_peer(to, c)).start()

    def second_done(k, to, frm):
        for c in (core, 1 - core):
            send(mid, cross.at[c, frm], s2.at[c, k], r2.at[c, frm], cross_peer(to, c)).wait()

    others(outer, second)
    send(mid, cross.at[core, outer], s2.at[1 - core, 0], r2.at[core, outer], partner).start()
    send(mid, cross.at[1 - core, outer], s2.at[1 - core, 0], r2.at[1 - core, outer], partner).wait()
    others(outer, second_done)
    mean = jnp.sum(cross[0], axis=0) / rows_total
    squares = jnp.sum(cross[1], axis=0) / rows_total
    out_ref[:8] = mean
    out_ref[8:] = lax.rsqrt(jnp.maximum(squares - jnp.square(mean), 0.0) + 1e-05)


def raw_features(points, marks, norms, hi, lo, rows_total):
    rows = points.shape[0]
    n = marks.shape[0]
    shape = (16, n // 8)
    return pl.pallas_call(
        functools.partial(raw_kernel, rows_total),
        out_shape=[jax.ShapeDtypeStruct((rows, n), F32), jax.ShapeDtypeStruct(shape, F32)],
        in_specs=[VMEM] * 5,
        out_specs=[VMEM, VMEM],
        scratch_shapes=[
            pltpu.VMEM((2, 8, n // 8), F32),
            pltpu.VMEM((8, n // 8), F32),
            pltpu.VMEM((16, 8, n // 8), F32),
            pltpu.VMEM((2, 16, 8, n // 8), F32),
        ]
        + [DMA((16,))] * 2
        + [DMA((2, 16))] * 2,
        name="raw",
        compiler_params=pltpu.CompilerParams(
            collective_id=1, has_side_effects=True, vmem_limit_bytes=40 << 20
        ),
    )(points, marks, norms, hi, lo)


def standardize_kernel(raw_ref, stats_ref, out_ref, buf, sems):
    steps = raw_ref.shape[0] // ROWS_STEP
    copies = []
    for s in range(steps):
        rows = slice(s * ROWS_STEP, (s + 1) * ROWS_STEP)
        if s >= 2:
            copies[s - 2].wait()
        for i in range(8):
            cols = slice(i * 128, (i + 1) * 128)
            x = raw_ref[rows, cols] - stats_ref[i : i + 1, :]
            buf[s % 2, :, cols] = (x * stats_ref[8 + i : 9 + i, :]).astype(BF16)
        copies.append(pltpu.make_async_copy(buf.at[s % 2], out_ref.at[rows, :], sems.at[s % 2]))
        copies[s].start()
    copies[steps - 2].wait()
    copies[steps - 1].wait()


def standardize(raw, stats):
    rows, n = raw.shape
    return pl.pallas_call(
        standardize_kernel,
        out_shape=jax.ShapeDtypeStruct((rows, n), BF16),
        in_specs=[VMEM, VMEM],
        out_specs=pl.BlockSpec(memory_space=pl.ANY),
        scratch_shapes=[pltpu.VMEM((2, ROWS_STEP, n), BF16), DMA((2,))],
        name="standardize",
        compiler_params=pltpu.CompilerParams(vmem_limit_bytes=16 << 20),
    )(raw, stats)


def shards(points, ridge, landmark_ids):
    marks = gather_marks(points, landmark_ids)
    hi, lo, norms = factor(marks, ridge)
    raw, stats = raw_features(points, marks, norms, hi, lo, points.shape[0] * lax.axis_size(GRP_DEV))
    return standardize(raw, stats)


def solution(mesh):
    torus = Mesh(
        mesh.devices.reshape(mesh.shape["grp"], 4, 8, 2), ("grp", "dev_0", "dev_1", "dev_2")
    )
    placed = (P(GRP_DEV, None), P(), P())
    return jax.shard_map(
        shards, mesh=torus, in_specs=placed, out_specs=P(GRP_DEV, None), check_vma=False
    )
```

```python
import functools

import jax
import jax.numpy as jnp
from jax import lax
from jax.experimental import pallas as pl
from jax.experimental.pallas import tpu as pltpu
from jax.sharding import Mesh
from jax.sharding import PartitionSpec as P

GRP_DEV = ("grp", "dev_0", "dev_1", "dev_2")
F32 = jnp.float32
BF16 = jnp.bfloat16
HI = lax.Precision.HIGHEST
BLK = 128
ROWS_STEP = 1024
OUT_STEP = 256
VMEM = pl.BlockSpec(memory_space=pltpu.VMEM)


def lane(x, c):
    return jnp.broadcast_to(x[:, c : c + 1], (8, 128))


def sub(x, k):
    return jnp.broadcast_to(x[k : k + 1, :], (8, 128))


def eliminate64(g1, g2, lane0):
    row = lax.broadcasted_iota(jnp.int32, (8, 128), 0)
    for q in range(8):
        b = [[lane(g1[t], lane0 + 8 * q + c) for t in range(q, 8)] for c in range(8)]
        root = None
        scale, inverse, last_scale, last_inverse = None, None, None, None
        for k in range(8):
            p = sub(b[k][0], k)
            r = 1.0 / p
            rs = lax.rsqrt(p if k == 0 else p * inverse)
            root = rs if k == 0 else jnp.where(row == k, rs, root)
            m = [x * r for x in b[k]]
            m[0] = jnp.where(row > k, m[0], 0.0)
            if k < 7:
                pc, bk = p, b[k]
                if last_inverse is not None:
                    pc, bk = p * last_inverse, [x * last_inverse for x in b[k]]
                for c in range(k + 1, 8):
                    a = sub(b[c][0], k)
                    b[c] = [pc * x - y * a for x, y in zip(b[c], bk)]
                if k == 0:
                    scale, inverse = p, r
                else:
                    next_inverse = inverse * r if last_scale is None else inverse * r * last_scale
                    scale, last_scale = scale * pc, scale
                    inverse, last_inverse = next_inverse, inverse
            a1 = sub(g1[q], k)
            a2 = sub(g2[q], k)
            for t in range(q, 8):
                g1[t] = g1[t] - m[t - q] * a1
                g2[t] = g2[t] - m[t - q] * a2
        g1[q] = g1[q] * root
        g2[q] = g2[q] * root
    return g1, g2


def split(x):
    high = x.astype(BF16)
    return high, (x - high.astype(F32)).astype(BF16)


def cat(xs, axis):
    return jnp.concatenate(xs, axis)


def pair_dot(a, high, low):
    return jnp.dot(a, high, preferred_element_type=F32) + jnp.dot(a, low, preferred_element_type=F32)


def inverse_factor(s, eye):
    rows = lambda x: [x[8 * t : 8 * t + 8] for t in range(8)]
    u, v = eliminate64(rows(s[:64]), rows(eye[:64]), 0)
    v = cat(v, 0)
    high, low = split(cat([cat(u, 0), v], 1))
    uh, ul = high[:, :BLK], low[:, :BLK]
    t = lax.dot_general(
        cat([uh, ul, uh, ul], 0),
        cat([high, high, low, low], 0),
        (((0,), (0,)), ((), ())),
        preferred_element_type=F32,
    )[64:]
    _, v2 = eliminate64(rows(s[64:] - t[:, :BLK]), rows(eye[64:] - t[:, BLK:]), 64)
    return cat([v] + v2, 0)


def factor_kernel(marks_ref, ridge_ref, hi_ref, lo_ref, norm_ref, m, diag, inv, rt, rh, rl):
    n, d = marks_ref.shape
    nb = n // BLK
    eye = (
        lax.broadcasted_iota(jnp.int32, (BLK, BLK), 0)
        == lax.broadcasted_iota(jnp.int32, (BLK, BLK), 1)
    ).astype(F32)
    column = lax.broadcasted_iota(jnp.int32, (BLK, n), 1)
    sq = jnp.square(marks_ref[...].astype(F32))
    nr = lax.dot_general(
        jnp.ones((8, d), F32), sq, (((1,), (1,)), ((), ())), preferred_element_type=F32, precision=HI
    )
    norm_ref[...] = nr

    def core_rows(i):
        rows = slice(i * BLK, (i + 1) * BLK)
        blk = marks_ref[rows, :]
        nc = jnp.sum(jnp.square(blk.astype(F32)), axis=1, keepdims=True)
        g = lax.dot_general(blk, marks_ref[...], (((1,), (1,)), ((), ())), preferred_element_type=F32)
        m[rows, :] = jnp.exp((2.0 * g - nc - nr[:1]) * (1.0 / (2.0 * d)))
        m[rows, rows] += eye * ridge_ref[:, rows]

    def finish_row(j):
        here = pl.ds(pl.multiple_of(j * BLK, BLK), BLK)
        m[here, here] = eye
        high, low = split(m[here, :])
        r = pair_dot(cat(split(inv[...]), 1), cat([high, high], 0), cat([low, low], 0))
        high, low = split(r)
        keep = column < (j + 1) * BLK
        hi_ref[here, :] = jnp.where(keep, high, jnp.zeros_like(high))
        lo_ref[here, :] = jnp.where(keep, low, jnp.zeros_like(low))
        return r, high, low

    def update_rows(j):
        here = pl.ds(pl.multiple_of(j * BLK, BLK), BLK)
        r, high, low = finish_row(j)
        rh[:BLK, :] = high
        rh[BLK:, :] = high
        rl[:BLK, :] = low
        rl[BLK:, :] = low
        for i in range(1, nb):
            rows = slice(i * BLK, (i + 1) * BLK)
            m[rows, here] = jnp.where(i > j, 0.0, m[rows, here])
            high, low = split(jnp.where(i > j, r[:, rows].T, 0.0))
            rt[rows, :BLK] = high
            rt[rows, BLK:] = low
        for i in range(1, nb):
            rows = slice(i * BLK, (i + 1) * BLK)
            m[rows, :] = m[rows, :] - pair_dot(rt[rows, :], rh[...], rl[...])

    def next_diagonal(j, linv):
        here = pl.ds(pl.multiple_of(j * BLK, BLK), BLK)
        after = pl.ds(pl.multiple_of(jnp.minimum(j + 1, nb - 1) * BLK, BLK), BLK)
        high, low = split(m[here, after])
        u = pair_dot(cat(split(linv), 1), cat([high, high], 0), cat([low, low], 0))
        high, low = split(u)
        t = u.T
        diag[...] = m[after, after] - pair_dot(
            cat(split(t), 1), cat([high, high], 0), cat([low, low], 0)
        )
        inv[...] = linv

    core_rows(0)
    linv = inverse_factor(m[:BLK, :BLK], eye)
    for i in range(1, nb):
        core_rows(i)
    next_diagonal(0, linv)

    def step(j, carry):
        linv = inverse_factor(diag[...], eye)
        update_rows(j - 1)
        next_diagonal(j, linv)
        return carry

    lax.fori_loop(1, nb, step, 0)
    finish_row(nb - 1)


def factor(marks, ridge):
    n = marks.shape[0]
    return pl.pallas_call(
        factor_kernel,
        out_shape=[
            jax.ShapeDtypeStruct((n, n), BF16),
            jax.ShapeDtypeStruct((n, n), BF16),
            jax.ShapeDtypeStruct((8, n), F32),
        ],
        in_specs=[VMEM, VMEM],
        out_specs=[VMEM, VMEM, VMEM],
        scratch_shapes=[
            pltpu.VMEM((n, n), F32),
            pltpu.VMEM((BLK, BLK), F32),
            pltpu.VMEM((BLK, BLK), F32),
            pltpu.VMEM((n, 2 * BLK), BF16),
            pltpu.VMEM((2 * BLK, n), BF16),
            pltpu.VMEM((2 * BLK, n), BF16),
        ],
        name="factor",
        compiler_params=pltpu.CompilerParams(vmem_limit_bytes=40 << 20),
    )(marks, ridge.reshape(1, n))


MESH_IDS = pl.DeviceIdType.MESH
SLOTS = 16
WINDOW = 128
DMA = pltpu.SemaphoreType.DMA


def position():
    inner = lax.axis_index("dev_1") * 2 + lax.axis_index("dev_2")
    outer = lax.axis_index("grp") * 4 + lax.axis_index("dev_0")
    return inner, outer


def inner_peer(i):
    return {"dev_1": lax.div(i, 2), "dev_2": lax.rem(i, 2)}


def outer_peer(o):
    return {"grp": lax.div(o, 4), "dev_0": lax.rem(o, 4)}


def others(me, body):
    for k in range(1, 16):
        body(k, lax.rem(me + k, 16), lax.rem(me + 16 - k, 16))


def greet(inner, outer):
    barrier = pltpu.get_barrier_semaphore()

    def inner_step(k, to, frm):
        pl.semaphore_signal(barrier, inc=1, device_id=inner_peer(to), device_id_type=MESH_IDS)

    def outer_step(k, to, frm):
        pl.semaphore_signal(barrier, inc=1, device_id=outer_peer(to), device_id_type=MESH_IDS)

    others(inner, inner_step)
    others(outer, outer_step)
    return barrier


def send(src, dst, send_sem, recv_sem, peer):
    return pltpu.make_async_remote_copy(
        src_ref=src, dst_ref=dst, send_sem=send_sem, recv_sem=recv_sem, device_id=peer, device_id_type=MESH_IDS
    )


def count_below(ids, starts):
    return jnp.sum((ids < starts).astype(F32), axis=1, keepdims=True).astype(jnp.int32)


def gather_kernel(
    ids_ref, turn_ref, points_ref, marks_ref, over_ref, rows, line, window, windows, hot, s1, r1, s2, r2, s3, r3
):
    inner, outer = position()
    core = lax.rem(inner, 2)
    barrier = greet(inner, outer)
    count, d = points_ref.shape
    n = marks_ref.shape[0]
    iota = lambda shape, axis: lax.broadcasted_iota(jnp.int32, shape, axis)
    ids = ids_ref[...]
    low, high = turn_ref[0:1, 0:1], turn_ref[1:2, 0:1]
    clip = lambda x: jnp.minimum(jnp.maximum(x, low), high)
    start = (outer * 16 + inner) * count
    first = clip(count_below(ids, jnp.full((1, n), start)))
    mark = iota((SLOTS, n), 1)
    wanted = (
        (mark - first == iota((SLOTS, n), 0)) & (ids >= start) & (ids < start + count) & (mark < high)
    )
    sel = jnp.sum(jnp.where(wanted, ids - start + 1, 0).astype(F32), axis=1, keepdims=True) - 1.0
    pick = (iota((SLOTS, count), 1).astype(F32) == sel).astype(BF16)
    picked = jnp.dot(pick, points_ref[...], preferred_element_type=F32).astype(BF16)
    rows[0] = picked[:, :128]
    rows[1] = picked[:, 128:]
    line[inner] = rows[core]
    at = clip(count_below(ids, (outer * 16 + iota((24, n), 0)) * count))
    slot = iota((1, 16 * SLOTS), 1)
    place, limit = slot, slot
    for i in range(16):
        own = (slot >= i * SLOTS) & (slot < (i + 1) * SLOTS)
        place = jnp.where(own, at[i : i + 1] + (slot - i * SLOTS), place)
        limit = jnp.where(own, at[i + 1 : i + 2], limit)
    place = jnp.where(place < limit, place - at[0:1], -1)
    pick = (iota((WINDOW, 16 * SLOTS), 0) == place).astype(BF16)
    lines = count_below(ids, iota((24, n), 0) * (16 * count))
    owned = jnp.zeros((256, 1), F32)
    for i in range(n // 128):
        part = ids[:, i * 128 : (i + 1) * 128]
        begin = iota((256, 128), 0) * count
        hit = ((part >= begin) & (part < begin + count)).astype(F32)
        owned = owned + hit
    owned = jnp.max(jnp.sum(owned, axis=1, keepdims=True), axis=0, keepdims=True)
    longest = jnp.max(lines[1:17] - lines[0:16], axis=0, keepdims=True)
    over = (owned > SLOTS) | (longest > WINDOW)
    over_ref[...] = jnp.broadcast_to(over.astype(jnp.int32), over_ref.shape)
    lines = clip(lines)
    pl.semaphore_wait(barrier, 30)

    def first_send(k, to, frm):
        send(rows.at[lax.rem(to, 2)], line.at[inner], s1.at[k], r1.at[inner], inner_peer(to)).start()

    def first_done(k, to, frm):
        send(rows.at[lax.rem(to, 2)], line.at[frm], s1.at[k], r1.at[frm], inner_peer(to)).wait()

    others(inner, first_send)
    slot = iota((1, WINDOW), 1)
    places = []
    for g in range(16):
        place = lines[g : g + 1] + slot
        places.append(jnp.where(place < lines[g + 1 : g + 2], place, -1))
    for i in range(n // 128):
        row = iota((128, WINDOW), 0) + i * 128
        hot[i * 128 : (i + 1) * 128, :] = cat([(row == place).astype(BF16) for place in places], 1)
    others(inner, first_done)
    compact = jnp.dot(pick, line[...].reshape(16 * SLOTS, 128), preferred_element_type=F32).astype(BF16)
    window[...] = compact
    windows[core, outer] = compact
    partner = {"dev_2": 1 - core}

    def second(k, to, frm):
        send(window, windows.at[core, outer], s2.at[k], r2.at[outer], outer_peer(to)).start()

    others(outer, second)
    send(window, windows.at[core, outer], s3.at[0], r3.at[outer], partner).start()

    def forward(k, to, frm):
        send(window, windows.at[core, frm], s2.at[k], r2.at[frm], outer_peer(to)).wait_recv()
        send(windows.at[core, frm], windows.at[core, frm], s3.at[k], r3.at[frm], partner).start()

    others(outer, forward)

    def last(k, to, frm):
        send(window, windows.at[core, frm], s2.at[k], r2.at[frm], outer_peer(to)).wait_send()
        copy = send(windows.at[1 - core, frm], windows.at[1 - core, frm], s3.at[k], r3.at[frm], partner)
        copy.wait_send()
        copy.wait_recv()

    copy = send(window, windows.at[1 - core, outer], s3.at[0], r3.at[outer], partner)
    copy.wait_send()
    copy.wait_recv()
    others(outer, last)
    source = cat([windows[0].reshape(16 * WINDOW, 128), windows[1].reshape(16 * WINDOW, 128)], 1)
    for i in range(n // 256):
        part = slice(i * 256, (i + 1) * 256)
        marks_ref[part, :] = jnp.dot(hot[part, :], source, preferred_element_type=F32).astype(BF16)


def gather_turn(ids, turn, points):
    d = points.shape[1]
    n = ids.shape[1]
    return pl.pallas_call(
        gather_kernel,
        out_shape=[jax.ShapeDtypeStruct((n, d), BF16), jax.ShapeDtypeStruct((8, 128), jnp.int32)],
        in_specs=[VMEM, VMEM, VMEM],
        out_specs=[VMEM, VMEM],
        scratch_shapes=[
            pltpu.VMEM((2, SLOTS, d // 2), BF16),
            pltpu.VMEM((16, SLOTS, d // 2), BF16),
            pltpu.VMEM((WINDOW, d // 2), BF16),
            pltpu.VMEM((2, 16, WINDOW, d // 2), BF16),
            pltpu.VMEM((n, 16 * WINDOW), BF16),
        ]
        + [DMA((16,))] * 6,
        name="gather",
        compiler_params=pltpu.CompilerParams(
            collective_id=0, has_side_effects=True, vmem_limit_bytes=24 << 20
        ),
    )(ids, turn, points)


def gather_marks(points, ids):
    n = ids.shape[0]
    ids = ids.reshape(1, n)
    place = jnp.arange(n, dtype=jnp.int32)[:, None]

    def turn(low, high):
        bounds = jnp.stack([low, high]).astype(jnp.int32)
        return gather_turn(ids, jnp.broadcast_to(bounds[:, None], (2, 128)), points)

    marks, over = turn(jnp.int32(0), jnp.int32(n))

    def again(state):
        low, marks = state
        fresh = turn(low, low + SLOTS)[0]
        return low + SLOTS, jnp.where((place >= low) & (place < low + SLOTS), fresh, marks)

    return lax.while_loop(lambda s: s[0] < n, again, (jnp.where(over[0, 0] > 0, 0, n), marks))[1]


def raw_kernel(
    rows_total, points_ref, marks_ref, norm_ref, hi_ref, lo_ref, raw_ref, out_ref, own, mid, line, cross, s1, r1, s2, r2
):
    inner, outer = position()
    core = lax.rem(inner, 2)
    barrier = greet(inner, outer)
    cross_peer = lambda o, c: {"grp": lax.div(o, 4), "dev_0": lax.rem(o, 4), "dev_2": c}

    def greet_cross(k, to, frm):
        pl.semaphore_signal(barrier, inc=1, device_id=cross_peer(to, 1 - core), device_id_type=MESH_IDS)

    others(outer, greet_cross)
    rows, d = points_ref.shape
    n = marks_ref.shape[0]
    own[...] = jnp.zeros_like(own)

    def block(i, carry):
        here = pl.ds(pl.multiple_of(i * ROWS_STEP, ROWS_STEP), ROWS_STEP)
        pts = points_ref[here, :]
        nc = jnp.sum(jnp.square(pts.astype(F32)), axis=1, keepdims=True)
        g = lax.dot_general(pts, marks_ref[...], (((1,), (1,)), ((), ())), preferred_element_type=F32)
        ch, cl = split(jnp.exp((2.0 * g - nc - norm_ref[:1, :]) * (1.0 / (2.0 * d))))
        for j in range(n // 256):
            cols = slice(j * 256, (j + 1) * 256)
            k = (j + 1) * 256
            mul = lambda a, b: lax.dot_general(
                a, b, (((1,), (1,)), ((), ())), preferred_element_type=F32
            )
            x = mul(ch[:, :k], hi_ref[cols, :k])
            x += mul(cl[:, :k], hi_ref[cols, :k])
            x += mul(ch[:, :k], lo_ref[cols, :k])
            raw_ref[here, cols] = x
            for h in range(2):
                y = x[:, h * 128 : (h + 1) * 128]
                r = 2 * j + h
                own[0, r : r + 1, :] += jnp.sum(y, axis=0, keepdims=True)
                own[1, r : r + 1, :] += jnp.sum(jnp.square(y), axis=0, keepdims=True)
        return carry

    lax.fori_loop(0, rows // ROWS_STEP, block, 0)
    line[inner] = own[core]
    pl.semaphore_wait(barrier, 45)

    def first(k, to, frm):
        send(own.at[lax.rem(to, 2)], line.at[inner], s1.at[k], r1.at[inner], inner_peer(to)).start()

    def first_done(k, to, frm):
        send(own.at[lax.rem(to, 2)], line.at[frm], s1.at[k], r1.at[frm], inner_peer(to)).wait()

    others(inner, first)
    others(inner, first_done)
    total = jnp.sum(line[...], axis=0)
    mid[...] = total
    cross[core, outer] = total
    partner = {"dev_2": 1 - core}

    def second(k, to, frm):
        for c in (core, 1 - core):
            send(mid, cross.at[core, outer], s2.at[c, k], r2.at[core, outer], cross_peer(to, c)).start()

    def second_done(k, to, frm):
        for c in (core, 1 - core):
            send(mid, cross.at[c, frm], s2.at[c, k], r2.at[c, frm], cross_peer(to, c)).wait()

    others(outer, second)
    send(mid, cross.at[core, outer], s2.at[1 - core, 0], r2.at[core, outer], partner).start()
    send(mid, cross.at[1 - core, outer], s2.at[1 - core, 0], r2.at[1 - core, outer], partner).wait()
    others(outer, second_done)
    mean = jnp.sum(cross[0], axis=0) / rows_total
    squares = jnp.sum(cross[1], axis=0) / rows_total
    out_ref[:8] = mean
    out_ref[8:] = lax.rsqrt(jnp.maximum(squares - jnp.square(mean), 0.0) + 1e-05)


def raw_features(points, marks, norms, hi, lo, rows_total):
    rows = points.shape[0]
    n = marks.shape[0]
    shape = (16, n // 8)
    return pl.pallas_call(
        functools.partial(raw_kernel, rows_total),
        out_shape=[jax.ShapeDtypeStruct((rows, n), F32), jax.ShapeDtypeStruct(shape, F32)],
        in_specs=[VMEM] * 5,
        out_specs=[VMEM, VMEM],
        scratch_shapes=[
            pltpu.VMEM((2, 8, n // 8), F32),
            pltpu.VMEM((8, n // 8), F32),
            pltpu.VMEM((16, 8, n // 8), F32),
            pltpu.VMEM((2, 16, 8, n // 8), F32),
        ]
        + [DMA((16,))] * 2
        + [DMA((2, 16))] * 2,
        name="raw",
        compiler_params=pltpu.CompilerParams(
            collective_id=1, has_side_effects=True, vmem_limit_bytes=40 << 20
        ),
    )(points, marks, norms, hi, lo)


def standardize_kernel(raw_ref, stats_ref, out_ref, buf, sems):
    steps = raw_ref.shape[0] // OUT_STEP
    copies = []
    for s in range(steps):
        rows = slice(s * OUT_STEP, (s + 1) * OUT_STEP)
        if s >= 2:
            copies[s - 2].wait()
        for i in range(8):
            cols = slice(i * 128, (i + 1) * 128)
            x = raw_ref[rows, cols] - stats_ref[i : i + 1, :]
            buf[s % 2, :, cols] = (x * stats_ref[8 + i : 9 + i, :]).astype(BF16)
        copies.append(pltpu.make_async_copy(buf.at[s % 2], out_ref.at[rows, :], sems.at[s % 2]))
        copies[s].start()
    copies[steps - 2].wait()
    copies[steps - 1].wait()


def standardize(raw, stats):
    rows, n = raw.shape
    return pl.pallas_call(
        standardize_kernel,
        out_shape=jax.ShapeDtypeStruct((rows, n), BF16),
        in_specs=[VMEM, VMEM],
        out_specs=pl.BlockSpec(memory_space=pl.ANY),
        scratch_shapes=[pltpu.VMEM((2, OUT_STEP, n), BF16), DMA((2,))],
        name="standardize",
        compiler_params=pltpu.CompilerParams(vmem_limit_bytes=16 << 20),
    )(raw, stats)


def shards(points, ridge, landmark_ids):
    marks = gather_marks(points, landmark_ids)
    hi, lo, norms = factor(marks, ridge)
    raw, stats = raw_features(points, marks, norms, hi, lo, points.shape[0] * lax.axis_size(GRP_DEV))
    return standardize(raw, stats)


def solution(mesh):
    torus = Mesh(
        mesh.devices.reshape(mesh.shape["grp"], 4, 8, 2), ("grp", "dev_0", "dev_1", "dev_2")
    )
    placed = (P(GRP_DEV, None), P(), P())
    return jax.shard_map(
        shards, mesh=torus, in_specs=placed, out_specs=P(GRP_DEV, None), check_vma=False
    )
```

```python
import functools

import jax
import jax.numpy as jnp
from jax import lax
from jax.experimental import pallas as pl
from jax.experimental.pallas import tpu as pltpu
from jax.sharding import Mesh
from jax.sharding import PartitionSpec as P

GRP_DEV = ("grp", "dev_0", "dev_1", "dev_2")
F32 = jnp.float32
BF16 = jnp.bfloat16
HI = lax.Precision.HIGHEST
BLK = 128
ROWS_STEP = 1024
OUT_STEP = 256
VMEM = pl.BlockSpec(memory_space=pltpu.VMEM)


def lane(x, c):
    return jnp.broadcast_to(x[:, c : c + 1], (8, 128))


def sub(x, k):
    return jnp.broadcast_to(x[k : k + 1, :], (8, 128))


def eliminate64(g1, g2, lane0):
    row = lax.broadcasted_iota(jnp.int32, (8, 128), 0)
    for q in range(8):
        b = [[lane(g1[t], lane0 + 8 * q + c) for t in range(q, 8)] for c in range(8)]
        root = None
        held = []
        scale, inverse, last_scale, last_inverse = None, None, None, None
        for k in range(8):
            p = sub(b[k][0], k)
            r = 1.0 / p
            rs = lax.rsqrt(p if k == 0 else p * inverse)
            root = rs if k == 0 else jnp.where(row == k, rs, root)
            m = [x * r for x in b[k]]
            m[0] = jnp.where(row > k, m[0], 0.0)
            if k < 7:
                pc, bk = p, b[k]
                if last_inverse is not None:
                    pc, bk = p * last_inverse, [x * last_inverse for x in b[k]]
                for c in range(k + 1, 8):
                    a = sub(b[c][0], k)
                    b[c] = [pc * x - y * a for x, y in zip(b[c], bk)]
                if k == 0:
                    scale, inverse = p, r
                else:
                    next_inverse = inverse * r if last_scale is None else inverse * r * last_scale
                    scale, last_scale = scale * pc, scale
                    inverse, last_inverse = next_inverse, inverse
            a1 = sub(g1[q], k)
            a2 = sub(g2[q], k)
            g1[q] = g1[q] - m[0] * a1
            g2[q] = g2[q] - m[0] * a2
            held.append((m, a1, a2))
        for t in range(q + 1, 8):
            for g, w in ((g1, 1), (g2, 2)):
                terms = [h[0][t - q] * h[w] for h in held]
                while len(terms) > 1:
                    terms = [x + y for x, y in zip(terms[::2], terms[1::2])]
                g[t] = g[t] - terms[0]
        g1[q] = g1[q] * root
        g2[q] = g2[q] * root
    return g1, g2


def split(x):
    high = x.astype(BF16)
    return high, (x - high.astype(F32)).astype(BF16)


def cat(xs, axis):
    return jnp.concatenate(xs, axis)


def pair_dot(a, high, low):
    return jnp.dot(a, high, preferred_element_type=F32) + jnp.dot(a, low, preferred_element_type=F32)


def inverse_factor(s, eye):
    rows = lambda x: [x[8 * t : 8 * t + 8] for t in range(8)]
    u, v = eliminate64(rows(s[:64]), rows(eye[:64]), 0)
    v = cat(v, 0)
    high, low = split(cat([cat(u, 0), v], 1))
    uh, ul = high[:, :BLK], low[:, :BLK]
    t = lax.dot_general(
        cat([uh, ul, uh, ul], 0),
        cat([high, high, low, low], 0),
        (((0,), (0,)), ((), ())),
        preferred_element_type=F32,
    )[64:]
    _, v2 = eliminate64(rows(s[64:] - t[:, :BLK]), rows(eye[64:] - t[:, BLK:]), 64)
    return cat([v] + v2, 0)


def factor_kernel(marks_ref, ridge_ref, hi_ref, lo_ref, norm_ref, m, diag, inv, rt, rh, rl):
    n, d = marks_ref.shape
    nb = n // BLK
    eye = (
        lax.broadcasted_iota(jnp.int32, (BLK, BLK), 0)
        == lax.broadcasted_iota(jnp.int32, (BLK, BLK), 1)
    ).astype(F32)
    column = lax.broadcasted_iota(jnp.int32, (BLK, n), 1)
    sq = jnp.square(marks_ref[...].astype(F32))
    nr = lax.dot_general(
        jnp.ones((8, d), F32), sq, (((1,), (1,)), ((), ())), preferred_element_type=F32, precision=HI
    )
    norm_ref[...] = nr

    def core_rows(i):
        rows = slice(i * BLK, (i + 1) * BLK)
        blk = marks_ref[rows, :]
        nc = jnp.sum(jnp.square(blk.astype(F32)), axis=1, keepdims=True)
        g = lax.dot_general(blk, marks_ref[...], (((1,), (1,)), ((), ())), preferred_element_type=F32)
        m[rows, :] = jnp.exp((2.0 * g - nc - nr[:1]) * (1.0 / (2.0 * d)))
        m[rows, rows] += eye * ridge_ref[:, rows]

    def finish_row(j):
        here = pl.ds(pl.multiple_of(j * BLK, BLK), BLK)
        m[here, here] = eye
        high, low = split(m[here, :])
        r = pair_dot(cat(split(inv[...]), 1), cat([high, high], 0), cat([low, low], 0))
        high, low = split(r)
        keep = column < (j + 1) * BLK
        hi_ref[here, :] = jnp.where(keep, high, jnp.zeros_like(high))
        lo_ref[here, :] = jnp.where(keep, low, jnp.zeros_like(low))
        return r, high, low

    def update_rows(j):
        here = pl.ds(pl.multiple_of(j * BLK, BLK), BLK)
        r, high, low = finish_row(j)
        rh[:BLK, :] = high
        rh[BLK:, :] = high
        rl[:BLK, :] = low
        rl[BLK:, :] = low
        for i in range(1, nb):
            rows = slice(i * BLK, (i + 1) * BLK)
            m[rows, here] = jnp.where(i > j, 0.0, m[rows, here])
            high, low = split(jnp.where(i > j, r[:, rows].T, 0.0))
            rt[rows, :BLK] = high
            rt[rows, BLK:] = low
        for i in range(1, nb):
            rows = slice(i * BLK, (i + 1) * BLK)
            m[rows, :] = m[rows, :] - pair_dot(rt[rows, :], rh[...], rl[...])

    def next_diagonal(j, linv):
        here = pl.ds(pl.multiple_of(j * BLK, BLK), BLK)
        after = pl.ds(pl.multiple_of(jnp.minimum(j + 1, nb - 1) * BLK, BLK), BLK)
        high, low = split(m[here, after])
        u = pair_dot(cat(split(linv), 1), cat([high, high], 0), cat([low, low], 0))
        high, low = split(u)
        t = u.T
        diag[...] = m[after, after] - pair_dot(
            cat(split(t), 1), cat([high, high], 0), cat([low, low], 0)
        )
        inv[...] = linv

    core_rows(0)
    linv = inverse_factor(m[:BLK, :BLK], eye)
    for i in range(1, nb):
        core_rows(i)
    next_diagonal(0, linv)

    def step(j, carry):
        linv = inverse_factor(diag[...], eye)
        update_rows(j - 1)
        next_diagonal(j, linv)
        return carry

    lax.fori_loop(1, nb, step, 0)
    finish_row(nb - 1)


def factor(marks, ridge):
    n = marks.shape[0]
    return pl.pallas_call(
        factor_kernel,
        out_shape=[
            jax.ShapeDtypeStruct((n, n), BF16),
            jax.ShapeDtypeStruct((n, n), BF16),
            jax.ShapeDtypeStruct((8, n), F32),
        ],
        in_specs=[VMEM, VMEM],
        out_specs=[VMEM, VMEM, VMEM],
        scratch_shapes=[
            pltpu.VMEM((n, n), F32),
            pltpu.VMEM((BLK, BLK), F32),
            pltpu.VMEM((BLK, BLK), F32),
            pltpu.VMEM((n, 2 * BLK), BF16),
            pltpu.VMEM((2 * BLK, n), BF16),
            pltpu.VMEM((2 * BLK, n), BF16),
        ],
        name="factor",
        compiler_params=pltpu.CompilerParams(vmem_limit_bytes=40 << 20),
    )(marks, ridge.reshape(1, n))


MESH_IDS = pl.DeviceIdType.MESH
SLOTS = 16
WINDOW = 128
SENT = 96
DMA = pltpu.SemaphoreType.DMA


def position():
    inner = lax.axis_index("dev_1") * 2 + lax.axis_index("dev_2")
    outer = lax.axis_index("grp") * 4 + lax.axis_index("dev_0")
    return inner, outer


def inner_peer(i):
    return {"dev_1": lax.div(i, 2), "dev_2": lax.rem(i, 2)}


def outer_peer(o):
    return {"grp": lax.div(o, 4), "dev_0": lax.rem(o, 4)}


def others(me, body):
    for k in range(1, 16):
        body(k, lax.rem(me + k, 16), lax.rem(me + 16 - k, 16))


def greet(inner, outer):
    barrier = pltpu.get_barrier_semaphore()

    def inner_step(k, to, frm):
        pl.semaphore_signal(barrier, inc=1, device_id=inner_peer(to), device_id_type=MESH_IDS)

    def outer_step(k, to, frm):
        pl.semaphore_signal(barrier, inc=1, device_id=outer_peer(to), device_id_type=MESH_IDS)

    others(inner, inner_step)
    others(outer, outer_step)
    return barrier


def send(src, dst, send_sem, recv_sem, peer):
    return pltpu.make_async_remote_copy(
        src_ref=src, dst_ref=dst, send_sem=send_sem, recv_sem=recv_sem, device_id=peer, device_id_type=MESH_IDS
    )


def count_below(ids, starts):
    return jnp.sum((ids < starts).astype(F32), axis=1, keepdims=True).astype(jnp.int32)


def gather_kernel(
    ids_ref, turn_ref, points_ref, marks_ref, over_ref, pts, rows, line, window, windows, hot, s0, s1, r1, s2, r2, s3, r3
):
    inner, outer = position()
    core = lax.rem(inner, 2)
    fetch = pltpu.make_async_copy(points_ref, pts, s0)
    fetch.start()
    barrier = greet(inner, outer)
    count, d = points_ref.shape
    n = marks_ref.shape[0]
    iota = lambda shape, axis: lax.broadcasted_iota(jnp.int32, shape, axis)
    ids = ids_ref[...]
    low, high = turn_ref[0:1, 0:1], turn_ref[1:2, 0:1]
    clip = lambda x: jnp.minimum(jnp.maximum(x, low), high)
    windows[:, :, SENT:, :] = jnp.zeros((2, 16, WINDOW - SENT, 128), BF16)
    start = (outer * 16 + inner) * count
    first = clip(count_below(ids, jnp.full((1, n), start)))
    mark = iota((SLOTS, n), 1)
    wanted = (
        (mark - first == iota((SLOTS, n), 0)) & (ids >= start) & (ids < start + count) & (mark < high)
    )
    sel = jnp.sum(jnp.where(wanted, ids - start + 1, 0).astype(F32), axis=1, keepdims=True) - 1.0
    pick = (iota((SLOTS, count), 1).astype(F32) == sel).astype(BF16)
    fetch.wait()
    picked = jnp.dot(pick, pts[...], preferred_element_type=F32).astype(BF16)
    rows[0] = picked[:, :128]
    rows[1] = picked[:, 128:]
    line[inner] = rows[core]
    at = clip(count_below(ids, (outer * 16 + iota((24, n), 0)) * count))
    slot = iota((1, 16 * SLOTS), 1)
    place, limit = slot, slot
    for i in range(16):
        own = (slot >= i * SLOTS) & (slot < (i + 1) * SLOTS)
        place = jnp.where(own, at[i : i + 1] + (slot - i * SLOTS), place)
        limit = jnp.where(own, at[i + 1 : i + 2], limit)
    place = jnp.where(place < limit, place - at[0:1], -1)
    pick = (iota((WINDOW, 16 * SLOTS), 0) == place).astype(BF16)
    lines = count_below(ids, iota((24, n), 0) * (16 * count))
    owned = jnp.zeros((256, 1), F32)
    for i in range(n // 128):
        part = ids[:, i * 128 : (i + 1) * 128]
        begin = iota((256, 128), 0) * count
        hit = ((part >= begin) & (part < begin + count)).astype(F32)
        owned = owned + hit
    owned = jnp.max(jnp.sum(owned, axis=1, keepdims=True), axis=0, keepdims=True)
    longest = jnp.max(lines[1:17] - lines[0:16], axis=0, keepdims=True)
    over = (owned > SLOTS) | (longest > SENT)
    over_ref[...] = jnp.broadcast_to(over.astype(jnp.int32), over_ref.shape)
    lines = clip(lines)
    pl.semaphore_wait(barrier, 30)

    def first_send(k, to, frm):
        send(rows.at[lax.rem(to, 2)], line.at[inner], s1.at[k], r1.at[inner], inner_peer(to)).start()

    def first_done(k, to, frm):
        send(rows.at[lax.rem(to, 2)], line.at[frm], s1.at[k], r1.at[frm], inner_peer(to)).wait()

    others(inner, first_send)
    slot = iota((1, WINDOW), 1)
    places = []
    for g in range(16):
        place = lines[g : g + 1] + slot
        places.append(jnp.where(place < lines[g + 1 : g + 2], place, -1))
    for i in range(n // 128):
        row = iota((128, WINDOW), 0) + i * 128
        hot[i * 128 : (i + 1) * 128, :] = cat([(row == place).astype(BF16) for place in places], 1)
    others(inner, first_done)
    compact = jnp.dot(pick, line[...].reshape(16 * SLOTS, 128), preferred_element_type=F32).astype(BF16)
    window[...] = compact
    windows[core, outer, :SENT] = compact[:SENT]
    kept = pl.ds(0, SENT)
    partner = {"dev_2": 1 - core}

    def second(k, to, frm):
        send(window.at[kept], windows.at[core, outer, kept], s2.at[k], r2.at[outer], outer_peer(to)).start()

    others(outer, second)
    send(window.at[kept], windows.at[core, outer, kept], s3.at[0], r3.at[outer], partner).start()

    def forward(k, to, frm):
        send(window.at[kept], windows.at[core, frm, kept], s2.at[k], r2.at[frm], outer_peer(to)).wait_recv()
        send(windows.at[core, frm, kept], windows.at[core, frm, kept], s3.at[k], r3.at[frm], partner).start()

    others(outer, forward)

    def last(k, to, frm):
        send(window.at[kept], windows.at[core, frm, kept], s2.at[k], r2.at[frm], outer_peer(to)).wait_send()
        copy = send(windows.at[1 - core, frm, kept], windows.at[1 - core, frm, kept], s3.at[k], r3.at[frm], partner)
        copy.wait_send()
        copy.wait_recv()

    copy = send(window.at[kept], windows.at[1 - core, outer, kept], s3.at[0], r3.at[outer], partner)
    copy.wait_send()
    copy.wait_recv()
    others(outer, last)
    source = cat([windows[0].reshape(16 * WINDOW, 128), windows[1].reshape(16 * WINDOW, 128)], 1)
    for i in range(n // 256):
        part = slice(i * 256, (i + 1) * 256)
        marks_ref[part, :] = jnp.dot(hot[part, :], source, preferred_element_type=F32).astype(BF16)


def gather_turn(ids, turn, points):
    d = points.shape[1]
    n = ids.shape[1]
    return pl.pallas_call(
        gather_kernel,
        out_shape=[jax.ShapeDtypeStruct((n, d), BF16), jax.ShapeDtypeStruct((8, 128), jnp.int32)],
        in_specs=[VMEM, VMEM, pl.BlockSpec(memory_space=pl.ANY)],
        out_specs=[VMEM, VMEM],
        scratch_shapes=[
            pltpu.VMEM(points.shape, BF16),
            pltpu.VMEM((2, SLOTS, d // 2), BF16),
            pltpu.VMEM((16, SLOTS, d // 2), BF16),
            pltpu.VMEM((WINDOW, d // 2), BF16),
            pltpu.VMEM((2, 16, WINDOW, d // 2), BF16),
            pltpu.VMEM((n, 16 * WINDOW), BF16),
            DMA,
        ]
        + [DMA((16,))] * 6,
        name="gather",
        compiler_params=pltpu.CompilerParams(
            collective_id=0, has_side_effects=True, vmem_limit_bytes=24 << 20
        ),
    )(ids, turn, points)


def gather_marks(points, ids):
    n = ids.shape[0]
    ids = ids.reshape(1, n)
    place = jnp.arange(n, dtype=jnp.int32)[:, None]

    def turn(low, high):
        bounds = jnp.stack([low, high]).astype(jnp.int32)
        return gather_turn(ids, jnp.broadcast_to(bounds[:, None], (2, 128)), points)

    marks, over = turn(jnp.int32(0), jnp.int32(n))

    def again(state):
        low, marks = state
        fresh = turn(low, low + SLOTS)[0]
        return low + SLOTS, jnp.where((place >= low) & (place < low + SLOTS), fresh, marks)

    return lax.while_loop(lambda s: s[0] < n, again, (jnp.where(over[0, 0] > 0, 0, n), marks))[1]


def raw_kernel(
    rows_total, points_ref, marks_ref, norm_ref, hi_ref, lo_ref, raw_ref, out_ref, own, mid, line, cross, s1, r1, s2, r2
):
    inner, outer = position()
    core = lax.rem(inner, 2)
    barrier = greet(inner, outer)
    cross_peer = lambda o, c: {"grp": lax.div(o, 4), "dev_0": lax.rem(o, 4), "dev_2": c}

    def greet_cross(k, to, frm):
        pl.semaphore_signal(barrier, inc=1, device_id=cross_peer(to, 1 - core), device_id_type=MESH_IDS)

    others(outer, greet_cross)
    rows, d = points_ref.shape
    n = marks_ref.shape[0]
    own[...] = jnp.zeros_like(own)

    def block(i, carry):
        here = pl.ds(pl.multiple_of(i * ROWS_STEP, ROWS_STEP), ROWS_STEP)
        pts = points_ref[here, :]
        nc = jnp.sum(jnp.square(pts.astype(F32)), axis=1, keepdims=True)
        g = lax.dot_general(pts, marks_ref[...], (((1,), (1,)), ((), ())), preferred_element_type=F32)
        ch, cl = split(jnp.exp((2.0 * g - nc - norm_ref[:1, :]) * (1.0 / (2.0 * d))))
        for j in range(n // 256):
            cols = slice(j * 256, (j + 1) * 256)
            k = (j + 1) * 256
            mul = lambda a, b: lax.dot_general(
                a, b, (((1,), (1,)), ((), ())), preferred_element_type=F32
            )
            x = mul(ch[:, :k], hi_ref[cols, :k])
            x += mul(cl[:, :k], hi_ref[cols, :k])
            x += mul(ch[:, :k], lo_ref[cols, :k])
            raw_ref[here, cols] = x
            for h in range(2):
                y = x[:, h * 128 : (h + 1) * 128]
                r = 2 * j + h
                own[0, r : r + 1, :] += jnp.sum(y, axis=0, keepdims=True)
                own[1, r : r + 1, :] += jnp.sum(jnp.square(y), axis=0, keepdims=True)
        return carry

    lax.fori_loop(0, rows // ROWS_STEP, block, 0)
    line[inner] = own[core]
    pl.semaphore_wait(barrier, 45)

    def first(k, to, frm):
        send(own.at[lax.rem(to, 2)], line.at[inner], s1.at[k], r1.at[inner], inner_peer(to)).start()

    def first_done(k, to, frm):
        send(own.at[lax.rem(to, 2)], line.at[frm], s1.at[k], r1.at[frm], inner_peer(to)).wait()

    others(inner, first)
    others(inner, first_done)
    total = jnp.sum(line[...], axis=0)
    mid[...] = total
    cross[core, outer] = total
    partner = {"dev_2": 1 - core}

    def second(k, to, frm):
        for c in (core, 1 - core):
            send(mid, cross.at[core, outer], s2.at[c, k], r2.at[core, outer], cross_peer(to, c)).start()

    def second_done(k, to, frm):
        for c in (core, 1 - core):
            send(mid, cross.at[c, frm], s2.at[c, k], r2.at[c, frm], cross_peer(to, c)).wait()

    others(outer, second)
    send(mid, cross.at[core, outer], s2.at[1 - core, 0], r2.at[core, outer], partner).start()
    send(mid, cross.at[1 - core, outer], s2.at[1 - core, 0], r2.at[1 - core, outer], partner).wait()
    others(outer, second_done)
    mean = jnp.sum(cross[0], axis=0) / rows_total
    squares = jnp.sum(cross[1], axis=0) / rows_total
    out_ref[:8] = mean
    out_ref[8:] = lax.rsqrt(jnp.maximum(squares - jnp.square(mean), 0.0) + 1e-05)


def raw_features(points, marks, norms, hi, lo, rows_total):
    rows = points.shape[0]
    n = marks.shape[0]
    shape = (16, n // 8)
    return pl.pallas_call(
        functools.partial(raw_kernel, rows_total),
        out_shape=[jax.ShapeDtypeStruct((rows, n), F32), jax.ShapeDtypeStruct(shape, F32)],
        in_specs=[VMEM] * 5,
        out_specs=[VMEM, VMEM],
        scratch_shapes=[
            pltpu.VMEM((2, 8, n // 8), F32),
            pltpu.VMEM((8, n // 8), F32),
            pltpu.VMEM((16, 8, n // 8), F32),
            pltpu.VMEM((2, 16, 8, n // 8), F32),
        ]
        + [DMA((16,))] * 2
        + [DMA((2, 16))] * 2,
        name="raw",
        compiler_params=pltpu.CompilerParams(
            collective_id=1, has_side_effects=True, vmem_limit_bytes=40 << 20
        ),
    )(points, marks, norms, hi, lo)


def standardize_kernel(raw_ref, stats_ref, out_ref, buf, sems):
    steps = raw_ref.shape[0] // OUT_STEP
    copies = []
    for s in range(steps):
        rows = slice(s * OUT_STEP, (s + 1) * OUT_STEP)
        if s >= 2:
            copies[s - 2].wait()
        for i in range(8):
            cols = slice(i * 128, (i + 1) * 128)
            x = raw_ref[rows, cols] - stats_ref[i : i + 1, :]
            buf[s % 2, :, cols] = (x * stats_ref[8 + i : 9 + i, :]).astype(BF16)
        copies.append(pltpu.make_async_copy(buf.at[s % 2], out_ref.at[rows, :], sems.at[s % 2]))
        copies[s].start()
    copies[steps - 2].wait()
    copies[steps - 1].wait()


def standardize(raw, stats):
    rows, n = raw.shape
    return pl.pallas_call(
        standardize_kernel,
        out_shape=jax.ShapeDtypeStruct((rows, n), BF16),
        in_specs=[VMEM, VMEM],
        out_specs=pl.BlockSpec(memory_space=pl.ANY),
        scratch_shapes=[pltpu.VMEM((2, OUT_STEP, n), BF16), DMA((2,))],
        name="standardize",
        compiler_params=pltpu.CompilerParams(vmem_limit_bytes=16 << 20),
    )(raw, stats)


def shards(points, ridge, landmark_ids):
    marks = gather_marks(points, landmark_ids)
    hi, lo, norms = factor(marks, ridge)
    raw, stats = raw_features(points, marks, norms, hi, lo, points.shape[0] * lax.axis_size(GRP_DEV))
    return standardize(raw, stats)


def solution(mesh):
    torus = Mesh(
        mesh.devices.reshape(mesh.shape["grp"], 4, 8, 2), ("grp", "dev_0", "dev_1", "dev_2")
    )
    placed = (P(GRP_DEV, None), P(), P())
    return jax.shard_map(
        shards, mesh=torus, in_specs=placed, out_specs=P(GRP_DEV, None), check_vma=False
    )
```

```python
import functools

import jax
import jax.numpy as jnp
from jax import lax
from jax.experimental import pallas as pl
from jax.experimental.pallas import tpu as pltpu
from jax.sharding import Mesh
from jax.sharding import PartitionSpec as P

GRP_DEV = ("grp", "dev_0", "dev_1", "dev_2")
F32 = jnp.float32
BF16 = jnp.bfloat16
HI = lax.Precision.HIGHEST
BLK = 128
ROWS_STEP = 1024
OUT_STEP = 256
VMEM = pl.BlockSpec(memory_space=pltpu.VMEM)


def lane(x, c):
    return jnp.broadcast_to(x[:, c : c + 1], (8, 128))


def sub(x, k):
    return jnp.broadcast_to(x[k : k + 1, :], (8, 128))


def eliminate64(g1, g2, lane0):
    row = lax.broadcasted_iota(jnp.int32, (8, 128), 0)
    for q in range(8):
        b = [[lane(g1[t], lane0 + 8 * q + c) for t in range(q, 8)] for c in range(8)]
        root = None
        held = []
        scale, inverse, last_scale, last_inverse = None, None, None, None
        for k in range(8):
            p = sub(b[k][0], k)
            r = 1.0 / p
            rs = lax.rsqrt(p if k == 0 else p * inverse)
            root = rs if k == 0 else jnp.where(row == k, rs, root)
            m = [x * r for x in b[k]]
            m[0] = jnp.where(row > k, m[0], 0.0)
            if k < 7:
                pc, bk = p, b[k]
                if last_inverse is not None:
                    pc, bk = p * last_inverse, [x * last_inverse for x in b[k]]
                for c in range(k + 1, 8):
                    a = sub(b[c][0], k)
                    b[c] = [pc * x - y * a for x, y in zip(b[c], bk)]
                if k == 0:
                    scale, inverse = p, r
                else:
                    next_inverse = inverse * r if last_scale is None else inverse * r * last_scale
                    scale, last_scale = scale * pc, scale
                    inverse, last_inverse = next_inverse, inverse
            a1 = sub(g1[q], k)
            a2 = sub(g2[q], k)
            g1[q] = g1[q] - m[0] * a1
            g2[q] = g2[q] - m[0] * a2
            held.append((m, a1, a2))
        for t in range(q + 1, 8):
            for g, w in ((g1, 1), (g2, 2)):
                terms = [h[0][t - q] * h[w] for h in held]
                while len(terms) > 1:
                    terms = [x + y for x, y in zip(terms[::2], terms[1::2])]
                g[t] = g[t] - terms[0]
        g1[q] = g1[q] * root
        g2[q] = g2[q] * root
    return g1, g2


def split(x):
    high = x.astype(BF16)
    return high, (x - high.astype(F32)).astype(BF16)


def cat(xs, axis):
    return jnp.concatenate(xs, axis)


def pair_dot(a, high, low):
    return jnp.dot(a, high, preferred_element_type=F32) + jnp.dot(a, low, preferred_element_type=F32)


def inverse_factor(s, eye):
    rows = lambda x: [x[8 * t : 8 * t + 8] for t in range(8)]
    u, v = eliminate64(rows(s[:64]), rows(eye[:64]), 0)
    v = cat(v, 0)
    high, low = split(cat([cat(u, 0), v], 1))
    uh, ul = high[:, :BLK], low[:, :BLK]
    t = lax.dot_general(
        cat([uh, ul, uh, ul], 0),
        cat([high, high, low, low], 0),
        (((0,), (0,)), ((), ())),
        preferred_element_type=F32,
    )[64:]
    _, v2 = eliminate64(rows(s[64:] - t[:, :BLK]), rows(eye[64:] - t[:, BLK:]), 64)
    return cat([v] + v2, 0)


def factor_kernel(marks_ref, ridge_ref, hi_ref, lo_ref, norm_ref, m, diag, inv, rt, rh, rl):
    n, d = marks_ref.shape
    nb = n // BLK
    eye = (
        lax.broadcasted_iota(jnp.int32, (BLK, BLK), 0)
        == lax.broadcasted_iota(jnp.int32, (BLK, BLK), 1)
    ).astype(F32)
    column = lax.broadcasted_iota(jnp.int32, (BLK, n), 1)
    sq = jnp.square(marks_ref[...].astype(F32))
    nr = lax.dot_general(
        jnp.ones((8, d), F32), sq, (((1,), (1,)), ((), ())), preferred_element_type=F32, precision=HI
    )
    norm_ref[...] = nr

    def core_rows(i):
        rows = slice(i * BLK, (i + 1) * BLK)
        blk = marks_ref[rows, :]
        nc = jnp.sum(jnp.square(blk.astype(F32)), axis=1, keepdims=True)
        g = lax.dot_general(blk, marks_ref[...], (((1,), (1,)), ((), ())), preferred_element_type=F32)
        m[rows, :] = jnp.exp((2.0 * g - nc - nr[:1]) * (1.0 / (2.0 * d)))
        m[rows, rows] += eye * ridge_ref[:, rows]

    def finish_row(j):
        here = pl.ds(pl.multiple_of(j * BLK, BLK), BLK)
        m[here, here] = eye
        high, low = split(m[here, :])
        r = pair_dot(cat(split(inv[...]), 1), cat([high, high], 0), cat([low, low], 0))
        high, low = split(r)
        keep = column < (j + 1) * BLK
        hi_ref[here, :] = jnp.where(keep, high, jnp.zeros_like(high))
        lo_ref[here, :] = jnp.where(keep, low, jnp.zeros_like(low))
        return r, high, low

    def update_rows(j):
        here = pl.ds(pl.multiple_of(j * BLK, BLK), BLK)
        r, high, low = finish_row(j)
        rh[:BLK, :] = high
        rh[BLK:, :] = high
        rl[:BLK, :] = low
        rl[BLK:, :] = low
        for i in range(1, nb):
            rows = slice(i * BLK, (i + 1) * BLK)
            m[rows, here] = jnp.where(i > j, 0.0, m[rows, here])
            high, low = split(jnp.where(i > j, r[:, rows].T, 0.0))
            rt[rows, :BLK] = high
            rt[rows, BLK:] = low
        for i in range(1, nb):
            rows = slice(i * BLK, (i + 1) * BLK)
            m[rows, :] = m[rows, :] - pair_dot(rt[rows, :], rh[...], rl[...])

    def next_diagonal(j, linv):
        here = pl.ds(pl.multiple_of(j * BLK, BLK), BLK)
        after = pl.ds(pl.multiple_of(jnp.minimum(j + 1, nb - 1) * BLK, BLK), BLK)
        high, low = split(m[here, after])
        u = pair_dot(cat(split(linv), 1), cat([high, high], 0), cat([low, low], 0))
        high, low = split(u)
        t = u.T
        diag[...] = m[after, after] - pair_dot(
            cat(split(t), 1), cat([high, high], 0), cat([low, low], 0)
        )
        inv[...] = linv

    core_rows(0)
    linv = inverse_factor(m[:BLK, :BLK], eye)
    for i in range(1, nb):
        core_rows(i)
    next_diagonal(0, linv)

    def step(j, carry):
        linv = inverse_factor(diag[...], eye)
        update_rows(j - 1)
        next_diagonal(j, linv)
        return carry

    lax.fori_loop(1, nb, step, 0)
    finish_row(nb - 1)


def factor(marks, ridge):
    n = marks.shape[0]
    return pl.pallas_call(
        factor_kernel,
        out_shape=[
            jax.ShapeDtypeStruct((n, n), BF16),
            jax.ShapeDtypeStruct((n, n), BF16),
            jax.ShapeDtypeStruct((8, n), F32),
        ],
        in_specs=[VMEM, VMEM],
        out_specs=[VMEM, VMEM, VMEM],
        scratch_shapes=[
            pltpu.VMEM((n, n), F32),
            pltpu.VMEM((BLK, BLK), F32),
            pltpu.VMEM((BLK, BLK), F32),
            pltpu.VMEM((n, 2 * BLK), BF16),
            pltpu.VMEM((2 * BLK, n), BF16),
            pltpu.VMEM((2 * BLK, n), BF16),
        ],
        name="factor",
        compiler_params=pltpu.CompilerParams(vmem_limit_bytes=40 << 20),
    )(marks, ridge)


MESH_IDS = pl.DeviceIdType.MESH
SLOTS = 16
WINDOW = 128
SENT = 96
DMA = pltpu.SemaphoreType.DMA


def position():
    inner = lax.axis_index("dev_1") * 2 + lax.axis_index("dev_2")
    outer = lax.axis_index("grp") * 4 + lax.axis_index("dev_0")
    return inner, outer


def inner_peer(i):
    return {"dev_1": lax.div(i, 2), "dev_2": lax.rem(i, 2)}


def outer_peer(o):
    return {"grp": lax.div(o, 4), "dev_0": lax.rem(o, 4)}


def others(me, body):
    for k in range(1, 16):
        body(k, lax.rem(me + k, 16), lax.rem(me + 16 - k, 16))


def greet(inner, outer):
    barrier = pltpu.get_barrier_semaphore()

    def inner_step(k, to, frm):
        pl.semaphore_signal(barrier, inc=1, device_id=inner_peer(to), device_id_type=MESH_IDS)

    def outer_step(k, to, frm):
        pl.semaphore_signal(barrier, inc=1, device_id=outer_peer(to), device_id_type=MESH_IDS)

    others(inner, inner_step)
    others(outer, outer_step)
    return barrier


def send(src, dst, send_sem, recv_sem, peer):
    return pltpu.make_async_remote_copy(
        src_ref=src, dst_ref=dst, send_sem=send_sem, recv_sem=recv_sem, device_id=peer, device_id_type=MESH_IDS
    )


def count_below(ids, starts):
    return jnp.sum((ids < starts).astype(F32), axis=1, keepdims=True).astype(jnp.int32)


def gather_kernel(
    ids_ref, turn_ref, points_ref, ridge_ref, marks_ref, over_ref, near_ref, pts, rows, line, window, windows, hot,
    s0, s1, r1, s2, r2, s3, r3
):
    inner, outer = position()
    core = lax.rem(inner, 2)
    fetch = pltpu.make_async_copy(points_ref, pts, s0.at[0])
    fetch.start()
    fetch_ridge = pltpu.make_async_copy(ridge_ref, near_ref, s0.at[1])
    fetch_ridge.start()
    barrier = greet(inner, outer)
    count, d = points_ref.shape
    n = marks_ref.shape[0]
    iota = lambda shape, axis: lax.broadcasted_iota(jnp.int32, shape, axis)
    ids = ids_ref[...]
    low, high = turn_ref[0:1, 0:1], turn_ref[1:2, 0:1]
    clip = lambda x: jnp.minimum(jnp.maximum(x, low), high)
    windows[:, :, SENT:, :] = jnp.zeros((2, 16, WINDOW - SENT, 128), BF16)
    start = (outer * 16 + inner) * count
    first = clip(count_below(ids, jnp.full((1, n), start)))
    mark = iota((SLOTS, n), 1)
    wanted = (
        (mark - first == iota((SLOTS, n), 0)) & (ids >= start) & (ids < start + count) & (mark < high)
    )
    sel = jnp.sum(jnp.where(wanted, ids - start + 1, 0).astype(F32), axis=1, keepdims=True) - 1.0
    pick = (iota((SLOTS, count), 1).astype(F32) == sel).astype(BF16)
    fetch.wait()
    fetch_ridge.wait()
    picked = jnp.dot(pick, pts[...], preferred_element_type=F32).astype(BF16)
    rows[0] = picked[:, :128]
    rows[1] = picked[:, 128:]
    line[inner] = rows[core]
    at = clip(count_below(ids, (outer * 16 + iota((24, n), 0)) * count))
    slot = iota((1, 16 * SLOTS), 1)
    place, limit = slot, slot
    for i in range(16):
        own = (slot >= i * SLOTS) & (slot < (i + 1) * SLOTS)
        place = jnp.where(own, at[i : i + 1] + (slot - i * SLOTS), place)
        limit = jnp.where(own, at[i + 1 : i + 2], limit)
    place = jnp.where(place < limit, place - at[0:1], -1)
    pick = (iota((WINDOW, 16 * SLOTS), 0) == place).astype(BF16)
    lines = count_below(ids, iota((24, n), 0) * (16 * count))
    owned = jnp.zeros((256, 1), F32)
    for i in range(n // 128):
        part = ids[:, i * 128 : (i + 1) * 128]
        begin = iota((256, 128), 0) * count
        hit = ((part >= begin) & (part < begin + count)).astype(F32)
        owned = owned + hit
    owned = jnp.max(jnp.sum(owned, axis=1, keepdims=True), axis=0, keepdims=True)
    longest = jnp.max(lines[1:17] - lines[0:16], axis=0, keepdims=True)
    over = (owned > SLOTS) | (longest > SENT)
    over_ref[...] = jnp.broadcast_to(over.astype(jnp.int32), over_ref.shape)
    lines = clip(lines)
    pl.semaphore_wait(barrier, 30)

    def first_send(k, to, frm):
        send(rows.at[lax.rem(to, 2)], line.at[inner], s1.at[k], r1.at[inner], inner_peer(to)).start()

    def first_done(k, to, frm):
        send(rows.at[lax.rem(to, 2)], line.at[frm], s1.at[k], r1.at[frm], inner_peer(to)).wait()

    others(inner, first_send)
    slot = iota((1, WINDOW), 1)
    places = []
    for g in range(16):
        place = lines[g : g + 1] + slot
        places.append(jnp.where(place < lines[g + 1 : g + 2], place, -1))
    for i in range(n // 128):
        row = iota((128, WINDOW), 0) + i * 128
        hot[i * 128 : (i + 1) * 128, :] = cat([(row == place).astype(BF16) for place in places], 1)
    others(inner, first_done)
    compact = jnp.dot(pick, line[...].reshape(16 * SLOTS, 128), preferred_element_type=F32).astype(BF16)
    window[...] = compact
    windows[core, outer, :SENT] = compact[:SENT]
    kept = pl.ds(0, SENT)
    partner = {"dev_2": 1 - core}

    def second(k, to, frm):
        send(window.at[kept], windows.at[core, outer, kept], s2.at[k], r2.at[outer], outer_peer(to)).start()

    others(outer, second)
    send(window.at[kept], windows.at[core, outer, kept], s3.at[0], r3.at[outer], partner).start()

    def forward(k, to, frm):
        send(window.at[kept], windows.at[core, frm, kept], s2.at[k], r2.at[frm], outer_peer(to)).wait_recv()
        send(windows.at[core, frm, kept], windows.at[core, frm, kept], s3.at[k], r3.at[frm], partner).start()

    others(outer, forward)

    def last(k, to, frm):
        send(window.at[kept], windows.at[core, frm, kept], s2.at[k], r2.at[frm], outer_peer(to)).wait_send()
        copy = send(windows.at[1 - core, frm, kept], windows.at[1 - core, frm, kept], s3.at[k], r3.at[frm], partner)
        copy.wait_send()
        copy.wait_recv()

    copy = send(window.at[kept], windows.at[1 - core, outer, kept], s3.at[0], r3.at[outer], partner)
    copy.wait_send()
    copy.wait_recv()
    others(outer, last)
    source = cat([windows[0].reshape(16 * WINDOW, 128), windows[1].reshape(16 * WINDOW, 128)], 1)
    for i in range(n // 256):
        part = slice(i * 256, (i + 1) * 256)
        marks_ref[part, :] = jnp.dot(hot[part, :], source, preferred_element_type=F32).astype(BF16)


def gather_turn(ids, turn, points, ridge):
    d = points.shape[1]
    n = ids.shape[1]
    return pl.pallas_call(
        gather_kernel,
        out_shape=[
            jax.ShapeDtypeStruct((n, d), BF16),
            jax.ShapeDtypeStruct((8, 128), jnp.int32),
            jax.ShapeDtypeStruct((1, n), F32),
        ],
        in_specs=[VMEM, VMEM, pl.BlockSpec(memory_space=pl.ANY), pl.BlockSpec(memory_space=pl.ANY)],
        out_specs=[VMEM, VMEM, VMEM],
        scratch_shapes=[
            pltpu.VMEM(points.shape, BF16),
            pltpu.VMEM((2, SLOTS, d // 2), BF16),
            pltpu.VMEM((16, SLOTS, d // 2), BF16),
            pltpu.VMEM((WINDOW, d // 2), BF16),
            pltpu.VMEM((2, 16, WINDOW, d // 2), BF16),
            pltpu.VMEM((n, 16 * WINDOW), BF16),
            DMA((2,)),
        ]
        + [DMA((16,))] * 6,
        name="gather",
        compiler_params=pltpu.CompilerParams(
            collective_id=0, has_side_effects=True, vmem_limit_bytes=24 << 20
        ),
    )(ids, turn, points, ridge)


def gather_marks(points, ids, ridge):
    n = ids.shape[0]
    ids = ids.reshape(1, n)
    ridge = ridge.reshape(1, n)
    place = jnp.arange(n, dtype=jnp.int32)[:, None]

    def turn(low, high):
        bounds = jnp.stack([low, high]).astype(jnp.int32)
        return gather_turn(ids, jnp.broadcast_to(bounds[:, None], (2, 128)), points, ridge)

    marks, over, near = turn(jnp.int32(0), jnp.int32(n))

    def again(state):
        low, marks = state
        fresh = turn(low, low + SLOTS)[0]
        return low + SLOTS, jnp.where((place >= low) & (place < low + SLOTS), fresh, marks)

    return lax.while_loop(lambda s: s[0] < n, again, (jnp.where(over[0, 0] > 0, 0, n), marks))[1], near


def raw_kernel(
    rows_total, points_ref, marks_ref, norm_ref, hi_ref, lo_ref, raw_ref, out_ref, own, mid, line, cross, s1, r1, s2, r2
):
    inner, outer = position()
    core = lax.rem(inner, 2)
    barrier = greet(inner, outer)
    cross_peer = lambda o, c: {"grp": lax.div(o, 4), "dev_0": lax.rem(o, 4), "dev_2": c}

    def greet_cross(k, to, frm):
        pl.semaphore_signal(barrier, inc=1, device_id=cross_peer(to, 1 - core), device_id_type=MESH_IDS)

    others(outer, greet_cross)
    rows, d = points_ref.shape
    n = marks_ref.shape[0]
    own[...] = jnp.zeros_like(own)

    def block(i, carry):
        here = pl.ds(pl.multiple_of(i * ROWS_STEP, ROWS_STEP), ROWS_STEP)
        pts = points_ref[here, :]
        nc = jnp.sum(jnp.square(pts.astype(F32)), axis=1, keepdims=True)
        g = lax.dot_general(pts, marks_ref[...], (((1,), (1,)), ((), ())), preferred_element_type=F32)
        ch, cl = split(jnp.exp((2.0 * g - nc - norm_ref[:1, :]) * (1.0 / (2.0 * d))))
        for j in range(n // 256):
            cols = slice(j * 256, (j + 1) * 256)
            k = (j + 1) * 256
            mul = lambda a, b: lax.dot_general(
                a, b, (((1,), (1,)), ((), ())), preferred_element_type=F32
            )
            x = mul(ch[:, :k], hi_ref[cols, :k])
            x += mul(cl[:, :k], hi_ref[cols, :k])
            x += mul(ch[:, :k], lo_ref[cols, :k])
            raw_ref[here, cols] = x
            for h in range(2):
                y = x[:, h * 128 : (h + 1) * 128]
                r = 2 * j + h
                own[0, r : r + 1, :] += jnp.sum(y, axis=0, keepdims=True)
                own[1, r : r + 1, :] += jnp.sum(jnp.square(y), axis=0, keepdims=True)
        return carry

    lax.fori_loop(0, rows // ROWS_STEP, block, 0)
    line[inner] = own[core]
    pl.semaphore_wait(barrier, 45)

    def first(k, to, frm):
        send(own.at[lax.rem(to, 2)], line.at[inner], s1.at[k], r1.at[inner], inner_peer(to)).start()

    def first_done(k, to, frm):
        send(own.at[lax.rem(to, 2)], line.at[frm], s1.at[k], r1.at[frm], inner_peer(to)).wait()

    others(inner, first)
    others(inner, first_done)
    total = jnp.sum(line[...], axis=0)
    mid[...] = total
    cross[core, outer] = total
    partner = {"dev_2": 1 - core}

    def second(k, to, frm):
        for c in (core, 1 - core):
            send(mid, cross.at[core, outer], s2.at[c, k], r2.at[core, outer], cross_peer(to, c)).start()

    def second_done(k, to, frm):
        for c in (core, 1 - core):
            send(mid, cross.at[c, frm], s2.at[c, k], r2.at[c, frm], cross_peer(to, c)).wait()

    others(outer, second)
    send(mid, cross.at[core, outer], s2.at[1 - core, 0], r2.at[core, outer], partner).start()
    send(mid, cross.at[1 - core, outer], s2.at[1 - core, 0], r2.at[1 - core, outer], partner).wait()
    others(outer, second_done)
    mean = jnp.sum(cross[0], axis=0) / rows_total
    squares = jnp.sum(cross[1], axis=0) / rows_total
    out_ref[:8] = mean
    out_ref[8:] = lax.rsqrt(jnp.maximum(squares - jnp.square(mean), 0.0) + 1e-05)


def raw_features(points, marks, norms, hi, lo, rows_total):
    rows = points.shape[0]
    n = marks.shape[0]
    shape = (16, n // 8)
    return pl.pallas_call(
        functools.partial(raw_kernel, rows_total),
        out_shape=[jax.ShapeDtypeStruct((rows, n), F32), jax.ShapeDtypeStruct(shape, F32)],
        in_specs=[VMEM] * 5,
        out_specs=[VMEM, VMEM],
        scratch_shapes=[
            pltpu.VMEM((2, 8, n // 8), F32),
            pltpu.VMEM((8, n // 8), F32),
            pltpu.VMEM((16, 8, n // 8), F32),
            pltpu.VMEM((2, 16, 8, n // 8), F32),
        ]
        + [DMA((16,))] * 2
        + [DMA((2, 16))] * 2,
        name="raw",
        compiler_params=pltpu.CompilerParams(
            collective_id=1, has_side_effects=True, vmem_limit_bytes=40 << 20
        ),
    )(points, marks, norms, hi, lo)


def standardize_kernel(raw_ref, stats_ref, out_ref, buf, sems):
    steps = raw_ref.shape[0] // OUT_STEP
    copies = []
    for s in range(steps):
        rows = slice(s * OUT_STEP, (s + 1) * OUT_STEP)
        if s >= 2:
            copies[s - 2].wait()
        for i in range(8):
            cols = slice(i * 128, (i + 1) * 128)
            x = raw_ref[rows, cols] - stats_ref[i : i + 1, :]
            buf[s % 2, :, cols] = (x * stats_ref[8 + i : 9 + i, :]).astype(BF16)
        copies.append(pltpu.make_async_copy(buf.at[s % 2], out_ref.at[rows, :], sems.at[s % 2]))
        copies[s].start()
    copies[steps - 2].wait()
    copies[steps - 1].wait()


def standardize(raw, stats):
    rows, n = raw.shape
    return pl.pallas_call(
        standardize_kernel,
        out_shape=jax.ShapeDtypeStruct((rows, n), BF16),
        in_specs=[VMEM, VMEM],
        out_specs=pl.BlockSpec(memory_space=pl.ANY),
        scratch_shapes=[pltpu.VMEM((2, OUT_STEP, n), BF16), DMA((2,))],
        name="standardize",
        compiler_params=pltpu.CompilerParams(vmem_limit_bytes=16 << 20),
    )(raw, stats)


def shards(points, ridge, landmark_ids):
    marks, ridge = gather_marks(points, landmark_ids, ridge)
    hi, lo, norms = factor(marks, ridge)
    raw, stats = raw_features(points, marks, norms, hi, lo, points.shape[0] * lax.axis_size(GRP_DEV))
    return standardize(raw, stats)


def solution(mesh):
    torus = Mesh(
        mesh.devices.reshape(mesh.shape["grp"], 4, 8, 2), ("grp", "dev_0", "dev_1", "dev_2")
    )
    placed = (P(GRP_DEV, None), P(), P())
    return jax.shard_map(
        shards, mesh=torus, in_specs=placed, out_specs=P(GRP_DEV, None), check_vma=False
    )
```

```python
import functools

import jax
import jax.numpy as jnp
from jax import lax
from jax.experimental import pallas as pl
from jax.experimental.pallas import tpu as pltpu
from jax.sharding import Mesh
from jax.sharding import PartitionSpec as P

GRP_DEV = ("grp", "dev_0", "dev_1", "dev_2")
F32 = jnp.float32
BF16 = jnp.bfloat16
HI = lax.Precision.HIGHEST
BLK = 128
ROWS_STEP = 512
OUT_STEP = 256
VMEM = pl.BlockSpec(memory_space=pltpu.VMEM)


def lane(x, c):
    return jnp.broadcast_to(x[:, c : c + 1], (8, 128))


def sub(x, k):
    return jnp.broadcast_to(x[k : k + 1, :], (8, 128))


def eliminate64(g1, g2, lane0):
    row = lax.broadcasted_iota(jnp.int32, (8, 128), 0)
    for q in range(8):
        b = [[lane(g1[t], lane0 + 8 * q + c) for t in range(q, 8)] for c in range(8)]
        root = None
        held = []
        scale, inverse, last_scale, last_inverse = None, None, None, None
        for k in range(8):
            p = sub(b[k][0], k)
            r = 1.0 / p
            rs = lax.rsqrt(p if k == 0 else p * inverse)
            root = rs if k == 0 else jnp.where(row == k, rs, root)
            m = [x * r for x in b[k]]
            m[0] = jnp.where(row > k, m[0], 0.0)
            if k < 7:
                pc, bk = p, b[k]
                if last_inverse is not None:
                    pc, bk = p * last_inverse, [x * last_inverse for x in b[k]]
                for c in range(k + 1, 8):
                    a = sub(b[c][0], k)
                    b[c] = [pc * x - y * a for x, y in zip(b[c], bk)]
                if k == 0:
                    scale, inverse = p, r
                else:
                    next_inverse = inverse * r if last_scale is None else inverse * r * last_scale
                    scale, last_scale = scale * pc, scale
                    inverse, last_inverse = next_inverse, inverse
            a1 = sub(g1[q], k)
            a2 = sub(g2[q], k)
            g1[q] = g1[q] - m[0] * a1
            g2[q] = g2[q] - m[0] * a2
            held.append((m, a1, a2))
        for t in range(q + 1, 8):
            for g, w in ((g1, 1), (g2, 2)):
                terms = [h[0][t - q] * h[w] for h in held]
                while len(terms) > 1:
                    terms = [x + y for x, y in zip(terms[::2], terms[1::2])]
                g[t] = g[t] - terms[0]
        g1[q] = g1[q] * root
        g2[q] = g2[q] * root
    return g1, g2


def split(x):
    high = x.astype(BF16)
    return high, (x - high.astype(F32)).astype(BF16)


def cat(xs, axis):
    return jnp.concatenate(xs, axis)


def pair_dot(a, high, low):
    return jnp.dot(a, high, preferred_element_type=F32) + jnp.dot(a, low, preferred_element_type=F32)


def inverse_factor(s, eye):
    rows = lambda x: [x[8 * t : 8 * t + 8] for t in range(8)]
    u, v = eliminate64(rows(s[:64]), rows(eye[:64]), 0)
    v = cat(v, 0)
    high, low = split(cat([cat(u, 0), v], 1))
    uh, ul = high[:, :BLK], low[:, :BLK]
    t = lax.dot_general(
        cat([uh, ul, uh, ul], 0),
        cat([high, high, low, low], 0),
        (((0,), (0,)), ((), ())),
        preferred_element_type=F32,
    )[64:]
    _, v2 = eliminate64(rows(s[64:] - t[:, :BLK]), rows(eye[64:] - t[:, BLK:]), 64)
    return cat([v] + v2, 0)


def factor_kernel(marks_ref, ridge_ref, hi_ref, lo_ref, norm_ref, m, diag, inv, rt, rh, rl):
    n, d = marks_ref.shape
    nb = n // BLK
    eye = (
        lax.broadcasted_iota(jnp.int32, (BLK, BLK), 0)
        == lax.broadcasted_iota(jnp.int32, (BLK, BLK), 1)
    ).astype(F32)
    column = lax.broadcasted_iota(jnp.int32, (BLK, n), 1)
    sq = jnp.square(marks_ref[...].astype(F32))
    nr = lax.dot_general(
        jnp.ones((8, d), F32), sq, (((1,), (1,)), ((), ())), preferred_element_type=F32, precision=HI
    )
    norm_ref[...] = nr

    def core_rows(i):
        rows = slice(i * BLK, (i + 1) * BLK)
        blk = marks_ref[rows, :]
        nc = jnp.sum(jnp.square(blk.astype(F32)), axis=1, keepdims=True)
        g = lax.dot_general(blk, marks_ref[...], (((1,), (1,)), ((), ())), preferred_element_type=F32)
        m[rows, :] = jnp.exp((2.0 * g - nc - nr[:1]) * (1.0 / (2.0 * d)))
        m[rows, rows] += eye * ridge_ref[:, rows]

    def finish_row(j):
        here = pl.ds(pl.multiple_of(j * BLK, BLK), BLK)
        m[here, here] = eye
        high, low = split(m[here, :])
        r = pair_dot(cat(split(inv[...]), 1), cat([high, high], 0), cat([low, low], 0))
        high, low = split(r)
        keep = column < (j + 1) * BLK
        hi_ref[here, :] = jnp.where(keep, high, jnp.zeros_like(high))
        lo_ref[here, :] = jnp.where(keep, low, jnp.zeros_like(low))
        return r, high, low

    def update_rows(j):
        here = pl.ds(pl.multiple_of(j * BLK, BLK), BLK)
        r, high, low = finish_row(j)
        rh[:BLK, :] = high
        rh[BLK:, :] = high
        rl[:BLK, :] = low
        rl[BLK:, :] = low
        for i in range(1, nb):
            rows = slice(i * BLK, (i + 1) * BLK)
            m[rows, here] = jnp.where(i > j, 0.0, m[rows, here])
            high, low = split(jnp.where(i > j, r[:, rows].T, 0.0))
            rt[rows, :BLK] = high
            rt[rows, BLK:] = low
        for i in range(1, nb):
            rows = slice(i * BLK, (i + 1) * BLK)
            m[rows, :] = m[rows, :] - pair_dot(rt[rows, :], rh[...], rl[...])

    def next_diagonal(j, linv):
        here = pl.ds(pl.multiple_of(j * BLK, BLK), BLK)
        after = pl.ds(pl.multiple_of(jnp.minimum(j + 1, nb - 1) * BLK, BLK), BLK)
        high, low = split(m[here, after])
        u = pair_dot(cat(split(linv), 1), cat([high, high], 0), cat([low, low], 0))
        high, low = split(u)
        t = u.T
        diag[...] = m[after, after] - pair_dot(
            cat(split(t), 1), cat([high, high], 0), cat([low, low], 0)
        )
        inv[...] = linv

    core_rows(0)
    linv = inverse_factor(m[:BLK, :BLK], eye)
    for i in range(1, nb):
        core_rows(i)
    next_diagonal(0, linv)

    def step(j, carry):
        linv = inverse_factor(diag[...], eye)
        update_rows(j - 1)
        next_diagonal(j, linv)
        return carry

    lax.fori_loop(1, nb, step, 0)
    finish_row(nb - 1)


def factor(marks, ridge):
    n = marks.shape[0]
    return pl.pallas_call(
        factor_kernel,
        out_shape=[
            jax.ShapeDtypeStruct((n, n), BF16),
            jax.ShapeDtypeStruct((n, n), BF16),
            jax.ShapeDtypeStruct((8, n), F32),
        ],
        in_specs=[VMEM, VMEM],
        out_specs=[VMEM, VMEM, VMEM],
        scratch_shapes=[
            pltpu.VMEM((n, n), F32),
            pltpu.VMEM((BLK, BLK), F32),
            pltpu.VMEM((BLK, BLK), F32),
            pltpu.VMEM((n, 2 * BLK), BF16),
            pltpu.VMEM((2 * BLK, n), BF16),
            pltpu.VMEM((2 * BLK, n), BF16),
        ],
        name="factor",
        compiler_params=pltpu.CompilerParams(vmem_limit_bytes=40 << 20),
    )(marks, ridge)


MESH_IDS = pl.DeviceIdType.MESH
SLOTS = 16
WINDOW = 128
SENT = 96
DMA = pltpu.SemaphoreType.DMA


def position():
    inner = lax.axis_index("dev_1") * 2 + lax.axis_index("dev_2")
    outer = lax.axis_index("grp") * 4 + lax.axis_index("dev_0")
    return inner, outer


def inner_peer(i):
    return {"dev_1": lax.div(i, 2), "dev_2": lax.rem(i, 2)}


def outer_peer(o):
    return {"grp": lax.div(o, 4), "dev_0": lax.rem(o, 4)}


def others(me, body):
    for k in range(1, 16):
        body(k, lax.rem(me + k, 16), lax.rem(me + 16 - k, 16))


def greet(inner, outer):
    barrier = pltpu.get_barrier_semaphore()

    def inner_step(k, to, frm):
        pl.semaphore_signal(barrier, inc=1, device_id=inner_peer(to), device_id_type=MESH_IDS)

    def outer_step(k, to, frm):
        pl.semaphore_signal(barrier, inc=1, device_id=outer_peer(to), device_id_type=MESH_IDS)

    others(inner, inner_step)
    others(outer, outer_step)
    return barrier


def send(src, dst, send_sem, recv_sem, peer):
    return pltpu.make_async_remote_copy(
        src_ref=src, dst_ref=dst, send_sem=send_sem, recv_sem=recv_sem, device_id=peer, device_id_type=MESH_IDS
    )


def count_below(ids, starts):
    return jnp.sum((ids < starts).astype(F32), axis=1, keepdims=True).astype(jnp.int32)


def gather_kernel(
    ids_ref, turn_ref, points_ref, ridge_ref, marks_ref, over_ref, near_ref, pts, rows, line, window, windows, hot,
    s0, s1, r1, s2, r2, s3, r3
):
    inner, outer = position()
    core = lax.rem(inner, 2)
    fetch = pltpu.make_async_copy(points_ref, pts, s0.at[0])
    fetch.start()
    fetch_ridge = pltpu.make_async_copy(ridge_ref, near_ref, s0.at[1])
    fetch_ridge.start()
    barrier = greet(inner, outer)
    count, d = points_ref.shape
    n = marks_ref.shape[0]
    iota = lambda shape, axis: lax.broadcasted_iota(jnp.int32, shape, axis)
    ids = ids_ref[...]
    low, high = turn_ref[0:1, 0:1], turn_ref[1:2, 0:1]
    clip = lambda x: jnp.minimum(jnp.maximum(x, low), high)
    windows[:, :, SENT:, :] = jnp.zeros((2, 16, WINDOW - SENT, 128), BF16)
    start = (outer * 16 + inner) * count
    first = clip(count_below(ids, jnp.full((1, n), start)))
    mark = iota((SLOTS, n), 1)
    wanted = (
        (mark - first == iota((SLOTS, n), 0)) & (ids >= start) & (ids < start + count) & (mark < high)
    )
    sel = jnp.sum(jnp.where(wanted, ids - start + 1, 0).astype(F32), axis=1, keepdims=True) - 1.0
    pick = (iota((SLOTS, count), 1).astype(F32) == sel).astype(BF16)
    fetch.wait()
    fetch_ridge.wait()
    picked = jnp.dot(pick, pts[...], preferred_element_type=F32).astype(BF16)
    rows[0] = picked[:, :128]
    rows[1] = picked[:, 128:]
    line[inner] = rows[core]
    at = clip(count_below(ids, (outer * 16 + iota((24, n), 0)) * count))
    slot = iota((1, 16 * SLOTS), 1)
    place, limit = slot, slot
    for i in range(16):
        own = (slot >= i * SLOTS) & (slot < (i + 1) * SLOTS)
        place = jnp.where(own, at[i : i + 1] + (slot - i * SLOTS), place)
        limit = jnp.where(own, at[i + 1 : i + 2], limit)
    place = jnp.where(place < limit, place - at[0:1], -1)
    pick = (iota((WINDOW, 16 * SLOTS), 0) == place).astype(BF16)
    lines = count_below(ids, iota((24, n), 0) * (16 * count))
    owned = jnp.zeros((256, 1), F32)
    for i in range(n // 128):
        part = ids[:, i * 128 : (i + 1) * 128]
        begin = iota((256, 128), 0) * count
        hit = ((part >= begin) & (part < begin + count)).astype(F32)
        owned = owned + hit
    owned = jnp.max(jnp.sum(owned, axis=1, keepdims=True), axis=0, keepdims=True)
    longest = jnp.max(lines[1:17] - lines[0:16], axis=0, keepdims=True)
    over = (owned > SLOTS) | (longest > SENT)
    over_ref[...] = jnp.broadcast_to(over.astype(jnp.int32), over_ref.shape)
    lines = clip(lines)
    pl.semaphore_wait(barrier, 30)

    def first_send(k, to, frm):
        send(rows.at[lax.rem(to, 2)], line.at[inner], s1.at[k], r1.at[inner], inner_peer(to)).start()

    def first_done(k, to, frm):
        send(rows.at[lax.rem(to, 2)], line.at[frm], s1.at[k], r1.at[frm], inner_peer(to)).wait()

    others(inner, first_send)
    slot = iota((1, WINDOW), 1)
    places = []
    for g in range(16):
        place = lines[g : g + 1] + slot
        places.append(jnp.where(place < lines[g + 1 : g + 2], place, -1))
    for i in range(n // 128):
        row = iota((128, WINDOW), 0) + i * 128
        hot[i * 128 : (i + 1) * 128, :] = cat([(row == place).astype(BF16) for place in places], 1)
    others(inner, first_done)
    compact = jnp.dot(pick, line[...].reshape(16 * SLOTS, 128), preferred_element_type=F32).astype(BF16)
    window[...] = compact
    windows[core, outer, :SENT] = compact[:SENT]
    kept = pl.ds(0, SENT)
    partner = {"dev_2": 1 - core}

    def second(k, to, frm):
        send(window.at[kept], windows.at[core, outer, kept], s2.at[k], r2.at[outer], outer_peer(to)).start()

    others(outer, second)
    send(window.at[kept], windows.at[core, outer, kept], s3.at[0], r3.at[outer], partner).start()

    def forward(k, to, frm):
        send(window.at[kept], windows.at[core, frm, kept], s2.at[k], r2.at[frm], outer_peer(to)).wait_recv()
        send(windows.at[core, frm, kept], windows.at[core, frm, kept], s3.at[k], r3.at[frm], partner).start()

    others(outer, forward)

    def last(k, to, frm):
        send(window.at[kept], windows.at[core, frm, kept], s2.at[k], r2.at[frm], outer_peer(to)).wait_send()
        copy = send(windows.at[1 - core, frm, kept], windows.at[1 - core, frm, kept], s3.at[k], r3.at[frm], partner)
        copy.wait_send()
        copy.wait_recv()

    copy = send(window.at[kept], windows.at[1 - core, outer, kept], s3.at[0], r3.at[outer], partner)
    copy.wait_send()
    copy.wait_recv()
    others(outer, last)
    source = cat([windows[0].reshape(16 * WINDOW, 128), windows[1].reshape(16 * WINDOW, 128)], 1)
    for i in range(n // 256):
        part = slice(i * 256, (i + 1) * 256)
        marks_ref[part, :] = jnp.dot(hot[part, :], source, preferred_element_type=F32).astype(BF16)


def gather_turn(ids, turn, points, ridge):
    d = points.shape[1]
    n = ids.shape[1]
    return pl.pallas_call(
        gather_kernel,
        out_shape=[
            jax.ShapeDtypeStruct((n, d), BF16),
            jax.ShapeDtypeStruct((8, 128), jnp.int32),
            jax.ShapeDtypeStruct((1, n), F32),
        ],
        in_specs=[VMEM, VMEM, pl.BlockSpec(memory_space=pl.ANY), pl.BlockSpec(memory_space=pl.ANY)],
        out_specs=[VMEM, VMEM, VMEM],
        scratch_shapes=[
            pltpu.VMEM(points.shape, BF16),
            pltpu.VMEM((2, SLOTS, d // 2), BF16),
            pltpu.VMEM((16, SLOTS, d // 2), BF16),
            pltpu.VMEM((WINDOW, d // 2), BF16),
            pltpu.VMEM((2, 16, WINDOW, d // 2), BF16),
            pltpu.VMEM((n, 16 * WINDOW), BF16),
            DMA((2,)),
        ]
        + [DMA((16,))] * 6,
        name="gather",
        compiler_params=pltpu.CompilerParams(
            collective_id=0, has_side_effects=True, vmem_limit_bytes=24 << 20
        ),
    )(ids, turn, points, ridge)


def gather_marks(points, ids, ridge):
    n = ids.shape[0]
    ids = ids.reshape(1, n)
    ridge = ridge.reshape(1, n)
    place = jnp.arange(n, dtype=jnp.int32)[:, None]

    def turn(low, high):
        bounds = jnp.stack([low, high]).astype(jnp.int32)
        return gather_turn(ids, jnp.broadcast_to(bounds[:, None], (2, 128)), points, ridge)

    marks, over, near = turn(jnp.int32(0), jnp.int32(n))

    def again(state):
        low, marks = state
        fresh = turn(low, low + SLOTS)[0]
        return low + SLOTS, jnp.where((place >= low) & (place < low + SLOTS), fresh, marks)

    return lax.while_loop(lambda s: s[0] < n, again, (jnp.where(over[0, 0] > 0, 0, n), marks))[1], near


def raw_kernel(
    rows_total, points_ref, marks_ref, norm_ref, hi_ref, lo_ref, raw_ref, out_ref, own, mid, line, cross, s1, r1, s2, r2
):
    inner, outer = position()
    core = lax.rem(inner, 2)
    barrier = greet(inner, outer)
    cross_peer = lambda o, c: {"grp": lax.div(o, 4), "dev_0": lax.rem(o, 4), "dev_2": c}

    def greet_cross(k, to, frm):
        pl.semaphore_signal(barrier, inc=1, device_id=cross_peer(to, 1 - core), device_id_type=MESH_IDS)

    others(outer, greet_cross)
    rows, d = points_ref.shape
    n = marks_ref.shape[0]
    own[...] = jnp.zeros_like(own)

    def block(i, carry):
        here = slice(i * ROWS_STEP, (i + 1) * ROWS_STEP)
        pts = points_ref[here, :]
        nc = jnp.sum(jnp.square(pts.astype(F32)), axis=1, keepdims=True)
        g = lax.dot_general(pts, marks_ref[...], (((1,), (1,)), ((), ())), preferred_element_type=F32)
        ch, cl = split(jnp.exp((2.0 * g - nc - norm_ref[:1, :]) * (1.0 / (2.0 * d))))
        for j in range(n // 256):
            cols = slice(j * 256, (j + 1) * 256)
            k = (j + 1) * 256
            mul = lambda a, b: lax.dot_general(
                a, b, (((1,), (1,)), ((), ())), preferred_element_type=F32
            )
            x = mul(ch[:, :k], hi_ref[cols, :k])
            x += mul(cl[:, :k], hi_ref[cols, :k])
            x += mul(ch[:, :k], lo_ref[cols, :k])
            raw_ref[here, cols] = x
            for h in range(2):
                y = x[:, h * 128 : (h + 1) * 128]
                r = 2 * j + h
                own[0, r : r + 1, :] += jnp.sum(y, axis=0, keepdims=True)
                own[1, r : r + 1, :] += jnp.sum(jnp.square(y), axis=0, keepdims=True)
        return carry

    for i in range(rows // ROWS_STEP):
        block(i, 0)
    line[inner] = own[core]
    pl.semaphore_wait(barrier, 45)

    def first(k, to, frm):
        send(own.at[lax.rem(to, 2)], line.at[inner], s1.at[k], r1.at[inner], inner_peer(to)).start()

    def first_done(k, to, frm):
        send(own.at[lax.rem(to, 2)], line.at[frm], s1.at[k], r1.at[frm], inner_peer(to)).wait()

    others(inner, first)
    others(inner, first_done)
    total = jnp.sum(line[...], axis=0)
    mid[...] = total
    cross[core, outer] = total
    partner = {"dev_2": 1 - core}

    def second(k, to, frm):
        for c in (core, 1 - core):
            send(mid, cross.at[core, outer], s2.at[c, k], r2.at[core, outer], cross_peer(to, c)).start()

    def second_done(k, to, frm):
        for c in (core, 1 - core):
            send(mid, cross.at[c, frm], s2.at[c, k], r2.at[c, frm], cross_peer(to, c)).wait()

    others(outer, second)
    send(mid, cross.at[core, outer], s2.at[1 - core, 0], r2.at[core, outer], partner).start()
    send(mid, cross.at[1 - core, outer], s2.at[1 - core, 0], r2.at[1 - core, outer], partner).wait()
    others(outer, second_done)
    mean = jnp.sum(cross[0], axis=0) / rows_total
    squares = jnp.sum(cross[1], axis=0) / rows_total
    out_ref[:8] = mean
    out_ref[8:] = lax.rsqrt(jnp.maximum(squares - jnp.square(mean), 0.0) + 1e-05)


def raw_features(points, marks, norms, hi, lo, rows_total):
    rows = points.shape[0]
    n = marks.shape[0]
    shape = (16, n // 8)
    return pl.pallas_call(
        functools.partial(raw_kernel, rows_total),
        out_shape=[jax.ShapeDtypeStruct((rows, n), F32), jax.ShapeDtypeStruct(shape, F32)],
        in_specs=[VMEM] * 5,
        out_specs=[VMEM, VMEM],
        scratch_shapes=[
            pltpu.VMEM((2, 8, n // 8), F32),
            pltpu.VMEM((8, n // 8), F32),
            pltpu.VMEM((16, 8, n // 8), F32),
            pltpu.VMEM((2, 16, 8, n // 8), F32),
        ]
        + [DMA((16,))] * 2
        + [DMA((2, 16))] * 2,
        name="raw",
        compiler_params=pltpu.CompilerParams(
            collective_id=1, has_side_effects=True, vmem_limit_bytes=40 << 20
        ),
    )(points, marks, norms, hi, lo)


def standardize_kernel(raw_ref, stats_ref, out_ref, buf, sems):
    steps = raw_ref.shape[0] // OUT_STEP
    copies = []
    for s in range(steps):
        rows = slice(s * OUT_STEP, (s + 1) * OUT_STEP)
        if s >= 2:
            copies[s - 2].wait()
        for i in range(8):
            cols = slice(i * 128, (i + 1) * 128)
            x = raw_ref[rows, cols] - stats_ref[i : i + 1, :]
            buf[s % 2, :, cols] = (x * stats_ref[8 + i : 9 + i, :]).astype(BF16)
        copies.append(pltpu.make_async_copy(buf.at[s % 2], out_ref.at[rows, :], sems.at[s % 2]))
        copies[s].start()
    copies[steps - 2].wait()
    copies[steps - 1].wait()


def standardize(raw, stats):
    rows, n = raw.shape
    return pl.pallas_call(
        standardize_kernel,
        out_shape=jax.ShapeDtypeStruct((rows, n), BF16),
        in_specs=[VMEM, VMEM],
        out_specs=pl.BlockSpec(memory_space=pl.ANY),
        scratch_shapes=[pltpu.VMEM((2, OUT_STEP, n), BF16), DMA((2,))],
        name="standardize",
        compiler_params=pltpu.CompilerParams(vmem_limit_bytes=16 << 20),
    )(raw, stats)


def shards(points, ridge, landmark_ids):
    marks, ridge = gather_marks(points, landmark_ids, ridge)
    hi, lo, norms = factor(marks, ridge)
    raw, stats = raw_features(points, marks, norms, hi, lo, points.shape[0] * lax.axis_size(GRP_DEV))
    return standardize(raw, stats)


def solution(mesh):
    torus = Mesh(
        mesh.devices.reshape(mesh.shape["grp"], 4, 8, 2), ("grp", "dev_0", "dev_1", "dev_2")
    )
    placed = (P(GRP_DEV, None), P(), P())
    return jax.shard_map(
        shards, mesh=torus, in_specs=placed, out_specs=P(GRP_DEV, None), check_vma=False
    )
```
